256 devices in a mesh: dp: 8 (over z_lo, y), space: 32 (over x, z_hi, core).
Axes of the slice: x: 4, y: 4, z: 8 (z_hi: 4, z_lo: 2; z = z_hi * 2 + z_lo), core: 2. Of those that a mesh axis runs over, the one named last changes fastest.
Arguments:
- volumes: bfloat16 [8, 128, 32, 4096], P('dp', 'space'), may hold values from -6 to 6
- first_filter: bfloat16 [3, 3, 3, 64, 128], replicated, may hold values from -0.15625 to 0.15625
- second_filter: bfloat16 [3, 3, 3, 128, 128], replicated, may hold values from -0.109375 to 0.109375
- upstream_grad: bfloat16 [8, 32, 8, 16, 128], P('dp', 'space'), may hold values from -0.029907227 to 0.029907227
Outputs:
- second_out: bfloat16 [8, 32, 8, 16, 128], P('dp', 'space')
- first_grad: float32 [3, 3, 3, 64, 128], P(None, None, None, None, 'space')
- second_grad: float32 [3, 3, 3, 128, 128], P(None, None, None, 'space')
The draws below stay inside these ranges and needn't reach their ends.
All inputs are finite; a program needn't handle non-finite values.
Results may differ from the reference program's by a relative error of at most 0.01.
The reference program's roundings to bfloat16 on the way (of `hidden`, `grad_pre_two`, `grad_hidden` and `grad_pre_one`) count: a program that leaves them out, or rounds other values in their place, can miss the bound.
Values may be sent and summed in bfloat16 or wider, within the bound.
No kernel may reach another device: no remote copies, remote signals or barrier semaphores. Data moves between devices by JAX's collectives and lax.ppermute only.
A program may use at most 64 MiB of HBM per device.

```python
import jax
import jax.numpy as jnp
from jax import lax

C0 = 64
C1 = 128
HEIGHT = 32
WIDTH = 64
B = 8
DEPTH = 128


def block_scale(own_key, dims, split, low, high):
    factor_of = 1.0
    for axis_at, blocks in split:
        heights = jax.random.uniform(jax.random.fold_in(jax.random.fold_in(own_key, 6), axis_at), (blocks,), jnp.float32, low / len(split), high / len(split))
        factor_of = factor_of * jnp.repeat(jnp.exp(heights), dims[axis_at] // blocks).reshape((-1,) + (1,) * (len(dims) - 1 - axis_at))
    return factor_of


def centred(rng, shape, scale, bound, shards=(), dtype=jnp.bfloat16):
    entries = scale * jax.random.normal(rng, shape, jnp.float32)
    if shards:
        entries = entries * block_scale(rng, shape, shards, -0.22, 0.18)
    return jnp.clip(entries, -bound, bound).astype(dtype)


def setup_inputs(seed: int = 0) -> dict:
    streams_of = jax.random.split(jax.random.key(seed), 5)
    return {
        "volumes": centred(streams_of[0], (B, DEPTH, HEIGHT, WIDTH * C0), 1.0, 6.0, ((0, 8), (1, 32))),
        "first_filter": centred(streams_of[1], (3, 3, 3, C0, C1), (27 * C0) ** -0.5, 0.15625),
        "second_filter": centred(streams_of[2], (3, 3, 3, C1, C1), (27 * C1) ** -0.5, 0.109375),
        "upstream_grad": centred(streams_of[3], (B, DEPTH // 4, HEIGHT // 4, WIDTH // 4, C1), 0.005, 0.029907227, ((0, 8), (1, 32))),
    }


SLOPE = 0.3

def leaky_relu(values):
    return jnp.where(values > 0, values, SLOPE * values)

def extract(volume, depth_pad):
    padded = jnp.pad(volume, ((0, 0), depth_pad, (1, 1), (1, 1), (0, 0)))
    depth_out = (padded.shape[1] - 3) // 2 + 1
    height_out = (padded.shape[2] - 3) // 2 + 1
    width_out = (padded.shape[3] - 3) // 2 + 1
    pieces = []
    for i in range(3):
        for j in range(3):
            for k in range(3):
                pieces.append(padded[:, i:i + 2 * depth_out - 1:2, j:j + 2 * height_out - 1:2, k:k + 2 * width_out - 1:2, :])
    return jnp.concatenate(pieces, axis=-1)

def spread(grads, shape, depth_pad):
    base = jnp.zeros(shape, jnp.float32)
    unused, pullback = jax.vjp(lambda volume: extract(volume, depth_pad), base)
    return pullback(grads)[0]

def flatten(values):
    return values.reshape(-1, values.shape[-1])

def contract_rows(left, right):
    return lax.dot_general(left, right, (((0,), (0,)), ((), ())), preferred_element_type=jnp.float32)

def reference(volumes, first_filter, second_filter, upstream_grad):
    first_flat = first_filter.reshape(27 * C0, C1)
    second_flat = second_filter.reshape(27 * C1, C1)

    def per_sample(carry, inputs):
        grad_one, grad_two = carry
        sample_volume, sample_grad = inputs
        volume_view = sample_volume.reshape(1, DEPTH, HEIGHT, WIDTH, C0)
        columns_one = extract(volume_view, (1, 1))
        shape_one = columns_one.shape[:-1]
        pre_one = jnp.dot(flatten(columns_one), first_flat, preferred_element_type=jnp.float32)
        hidden = leaky_relu(pre_one).astype(jnp.bfloat16).reshape(shape_one + (C1,))
        columns_two = extract(hidden, (1, 1))
        shape_two = columns_two.shape[:-1]
        pre_two = jnp.dot(flatten(columns_two), second_flat, preferred_element_type=jnp.float32).reshape(shape_two + (C1,))
        second_out = leaky_relu(pre_two).astype(jnp.bfloat16)
        grad_pre_two = (sample_grad[None].astype(jnp.float32) * jnp.where(pre_two > 0, 1.0, SLOPE)).astype(jnp.bfloat16)
        grad_two = grad_two + contract_rows(flatten(columns_two), flatten(grad_pre_two))
        grad_columns = lax.dot_general(flatten(grad_pre_two), second_flat, (((1,), (1,)), ((), ())), preferred_element_type=jnp.float32)
        grad_hidden = spread(grad_columns.reshape(shape_two + (27 * C1,)), hidden.shape, (1, 1)).astype(jnp.bfloat16)
        grad_pre_one = (grad_hidden.astype(jnp.float32) * jnp.where(hidden > 0, 1.0, SLOPE)).astype(jnp.bfloat16)
        grad_one = grad_one + contract_rows(flatten(columns_one), flatten(grad_pre_one))
        return ((grad_one, grad_two), second_out[0])
    start = (jnp.zeros((27 * C0, C1), jnp.float32), jnp.zeros((27 * C1, C1), jnp.float32))
    (grad_one, grad_two), second_out = lax.scan(per_sample, start, (volumes, upstream_grad))
    return (second_out, grad_one.reshape(3, 3, 3, C0, C1), grad_two.reshape(3, 3, 3, C1, C1))
```

```python
import jax
import jax.numpy as jnp
from jax import lax
from jax.experimental import pallas as pl
from jax.experimental.pallas import tpu as pltpu
from jax.sharding import PartitionSpec as P

SLOPE = 0.3
F32, BF16 = jnp.float32, jnp.bfloat16
FIRST_LANES = 14 * 128
SECOND_LANES = 27 * 128


def next_in_space(value, by):
    pairs = [(i, i + by) for i in range(32) if 0 <= i + by < 32]
    return lax.ppermute(value, "space", pairs)


def swap_core(value):
    return lax.ppermute(value, "space", [(i, i ^ 1) for i in range(32)])


def ring_x(value, k):
    return lax.ppermute(value, "space", [(i, ((i >> 3) + k) % 4 * 8 + (i & 7)) for i in range(32)])


def ring_z(value, k):
    return lax.ppermute(
        value, "space", [(i, (i & ~6) | ((((i >> 1) & 3) + k) % 4 << 1)) for i in range(32)]
    )


def ring_y(value, k):
    return lax.ppermute(value, "dp", [(i, (i & 4) | ((i & 3) + k) % 4) for i in range(8)])


def swap_z_low(value):
    return lax.ppermute(value, "dp", [(i, i ^ 4) for i in range(8)])


def leaky(values):
    return jnp.where(values > 0, values, SLOPE * values)


def dot(a, b):
    return jnp.dot(a, b, preferred_element_type=F32)


def dot_nt(a, b):
    return lax.dot_general(a, b, (((1,), (1,)), ((), ())), preferred_element_type=F32)


def rows_by_tap():
    m = lax.broadcasted_iota(jnp.int32, (48, 32), 0)
    h = lax.broadcasted_iota(jnp.int32, (48, 32), 1)
    return jnp.where(h == 2 * (m & 15) + (m >> 4) - 1, 1.0, 0.0).astype(BF16)


def channel_order():
    m = lax.broadcasted_iota(jnp.int32, (128, 128), 0)
    i = lax.broadcasted_iota(jnp.int32, (128, 128), 1)
    natural = ((m >> 4) & 3) * 32 + ((m >> 2) & 3) * 8 + (m >> 6) * 4 + (m & 3)
    return jnp.where(i == natural, 1.0, 0.0).astype(BF16)


def spread_rows(plane_ref, pick, y_ref):
    for t in range(3):
        y_ref[t, 0] = jnp.zeros((16, 128), BF16)
    for n in range(8):
        out = dot(pick, plane_ref[:, n * 512 : (n + 1) * 512]).astype(BF16)
        for t in range(3):
            for r in range(4):
                y_ref[t, 1 + 4 * n + r] = out[16 * t : 16 * t + 16, 128 * r : 128 * r + 128]


def columns(y_ref, b):
    before = y_ref[b, 0:32].reshape(512, 128)
    at = y_ref[b, 1:33].reshape(512, 128)
    return jnp.concatenate([before, at], axis=1)


def first_conv(planes, f_ref, w_ref):
    for ab in range(9):
        w_ref[ab * 256 : ab * 256 + 64] = jnp.zeros((64, 128), BF16)
        w_ref[ab * 256 + 64 : ab * 256 + 256] = f_ref[ab]
    lhs = jnp.concatenate([columns(planes[a], b) for a in range(3) for b in range(3)], axis=1)
    return leaky(dot(lhs, w_ref[...])).astype(BF16)


def core_x_z():
    s = lax.axis_index("space")
    return s & 1, s >> 3, (s >> 1) & 3


def upper_plane_kernel(v_ref, f_ref, y_ref, hid_ref, w_ref):
    pick = rows_by_tap()
    for p in range(4):
        spread_rows(v_ref.at[p], pick, y_ref.at[p])
    hid_ref[...] = first_conv([y_ref.at[p] for p in (1, 2, 3)], f_ref, w_ref)


def lower_plane_kernel(v_ref, y_ref, f_ref, yh_ref, hid_ref, w_ref):
    spread_rows(v_ref, rows_by_tap(), yh_ref)
    hid_ref[...] = first_conv([yh_ref, y_ref.at[0], y_ref.at[1]], f_ref, w_ref)


def second_conv_kernel(hm_ref, h0_ref, h1_ref, f_ref, up_ref, out_ref, gp_ref, t_ref, hs, us, os):
    for a, h_ref in enumerate((hm_ref, h0_ref, h1_ref)):
        h = h_ref[...].astype(F32).reshape(16, 2, 16, 128)
        hs[a, :, :, 0:8, :] = jnp.zeros((17, 2, 8, 128), F32)
        hs[a, 0, 0] = jnp.zeros((24, 128), F32)
        hs[a, 0:16, 1, 8:24, :] = h[:, 0]
        hs[a, 1:17, 0, 8:24, :] = h[:, 1]
    tap = 0
    for a in range(3):
        for b in range(3):
            for c in range(3):
                rows = hs[a, c // 2 : c // 2 + 16, c % 2, pl.ds(7 + b, 8, stride=2), :]
                t_ref[:, tap * 128 : tap * 128 + 128] = rows.reshape(128, 128).astype(BF16)
                tap += 1
    pre = dot(t_ref[...], f_ref[...])
    us[...] = up_ref[...].astype(F32).reshape(128, 128)
    up = jnp.concatenate([us[pl.ds(r, 8, stride=16), :] for r in range(16)], axis=0)
    gp_ref[...] = (up * jnp.where(pre > 0, 1.0, SLOPE)).astype(BF16)
    out = leaky(pre)
    for r in range(16):
        os[pl.ds(r, 8, stride=16), :] = out[8 * r : 8 * r + 8]
    out_ref[...] = os[...].astype(BF16).reshape(8, 16, 128)


def second_grad_kernel(t_ref, gp_ref, keep_ref, send_ref, g):
    order = channel_order()
    gp = gp_ref[...]
    for tap in range(27):
        lanes = slice(tap * 128, tap * 128 + 128)
        turned = dot_nt(order, t_ref[:, lanes]).astype(BF16)
        g[:, lanes] = dot(turned, gp)
    core, _, _ = core_x_z()
    keep_ref[...] = g[pl.ds(pl.multiple_of(core * 64, 64), 64), :]
    send_ref[...] = g[pl.ds(pl.multiple_of((1 - core) * 64, 64), 64), :].astype(BF16)


def first_grad_kernel(
    gp_ref, gpn_ref, f_ref, h0_ref, h1_ref, yh_ref, y_ref, keep_ref, send_ref, gs, gu, g
):
    gs[...] = jnp.zeros_like(gs)
    for s, ref in enumerate((gp_ref, gpn_ref)):
        gs[s, 0:16, 0:8, :] = ref[...].astype(F32).reshape(16, 8, 128)
    moved = {
        (s, dr, dq): gs[s, dr : dr + 16, dq : dq + 8, :].reshape(128, 128).astype(BF16)
        for s in range(2)
        for dr in range(2)
        for dq in range(2)
    }
    one_d = {0: [(0, 1)], 1: [(0, 2), (1, 0)]}
    for pu in range(2):
        for pv in range(2):
            for pw in range(2):
                lhs, rhs = [], []
                for s, a in one_d[pu]:
                    for dq, b in one_d[pv]:
                        for dr, c in one_d[pw]:
                            lhs.append(moved[s, dr, dq])
                            rhs.append(f_ref[9 * a + 3 * b + c])
                grad = dot_nt(jnp.concatenate(lhs, axis=1), jnp.concatenate(rhs, axis=1))
                grad = grad.astype(BF16).astype(F32).reshape(16, 8, 128)
                gu[pu, :, pw, pl.ds(pv, 8, stride=2), :] = grad
    grads = []
    for pu, h_ref in enumerate((h0_ref, h1_ref)):
        hid = h_ref[...].astype(F32)
        grads.append((gu[pu].reshape(512, 128) * jnp.where(hid > 0, 1.0, SLOPE)).astype(BF16))
    turned = dot_nt(channel_order(), jnp.concatenate(grads, axis=0)).astype(BF16)
    planes = [yh_ref] + [y_ref.at[p] for p in range(4)]
    low = lax.broadcasted_iota(jnp.int32, (128, 128), 1) < 64
    held = None
    for a in range(3):
        for b in range(3):
            ab = 3 * a + b
            rhs = jnp.concatenate([columns(planes[a], b), columns(planes[a + 2], b)], axis=0)
            grad = dot(turned, rhs)
            g[:, ab * 128 : ab * 128 + 128] = grad[:, 128:]
            if ab % 2 == 0:
                held = pltpu.roll(grad[:, :128], 64, axis=1)
            if ab % 2 == 1 or ab == 8:
                block = 9 + ab // 2
                upper = grad[:, :128] if ab % 2 else jnp.zeros_like(held)
                g[:, block * 128 : block * 128 + 128] = jnp.where(low, held, upper)
    core, _, _ = core_x_z()
    keep_ref[...] = g[pl.ds(pl.multiple_of(core * 64, 64), 64), :]
    send_ref[...] = g[pl.ds(pl.multiple_of((1 - core) * 64, 64), 64), :].astype(BF16)


def after_core_kernel(keep_ref, got_ref, own_ref, s1_ref, s2_ref, s3_ref, acc):
    acc[...] = keep_ref[...] + got_ref[...].astype(F32)
    _, x, _ = core_x_z()
    own_ref[...] = acc[pl.ds(pl.multiple_of(x * 16, 16), 16), :]
    for k, ref in enumerate((s1_ref, s2_ref, s3_ref)):
        at = pl.multiple_of(((x + k + 1) & 3) * 16, 16)
        ref[...] = acc[pl.ds(at, 16), :].astype(BF16)


def after_x_kernel(k1, a1, b1, c1, k2, a2, b2, c2, own_ref, s1_ref, s2_ref, s3_ref, acc):
    for start, refs in ((0, (k1, a1, b1, c1)), (FIRST_LANES, (k2, a2, b2, c2))):
        total = refs[0][...]
        for ref in refs[1:]:
            total = total + ref[...].astype(F32)
        for z in range(4):
            acc[z, :, start : start + total.shape[1]] = total[4 * z : 4 * z + 4]
    _, _, z = core_x_z()
    own_ref[...] = acc[z]
    for k, ref in enumerate((s1_ref, s2_ref, s3_ref)):
        ref[...] = acc[(z + k + 1) & 3].astype(BF16)


def after_z_kernel(own_ref, a_ref, b_ref, c_ref, out_ref):
    total = own_ref[...]
    for ref in (a_ref, b_ref, c_ref):
        total = total + ref[...].astype(F32)
    out_ref[...] = total.astype(BF16)


def after_y_kernel(own_ref, a_ref, b_ref, c_ref, out_ref):
    own, a, b, c = (ref[...].astype(F32) for ref in (own_ref, a_ref, b_ref, c_ref))
    out_ref[...] = ((own + b) + (a + c)).astype(BF16)


def final_kernel(own_ref, got_ref, first_ref, second_ref):
    total = own_ref[...].astype(F32) + got_ref[...].astype(F32)
    for ab in range(9):
        block = total[:, ab * 128 : ab * 128 + 128]
        first_ref[3 * ab + 1] = block[:, :64]
        first_ref[3 * ab + 2] = block[:, 64:]
        at = (9 + ab // 2) * 128 + (ab % 2) * 64
        first_ref[3 * ab] = total[:, at : at + 64]
    for tap in range(27):
        at = FIRST_LANES + tap * 128
        second_ref[tap] = total[:, at : at + 128]


def call(kernel, outs, *args, scratch=(), flops=0):
    size = sum(a.size * a.dtype.itemsize for a in args)
    return pl.pallas_call(
        kernel,
        out_shape=[jax.ShapeDtypeStruct(shape, dtype) for shape, dtype in outs],
        in_specs=[pl.BlockSpec(memory_space=pltpu.VMEM)] * len(args),
        out_specs=[pl.BlockSpec(memory_space=pltpu.VMEM)] * len(outs),
        scratch_shapes=[pltpu.VMEM(shape, dtype) for shape, dtype in scratch],
        compiler_params=pltpu.CompilerParams(vmem_limit_bytes=24 << 20),
        cost_estimate=pl.CostEstimate(flops=flops, bytes_accessed=size, transcendentals=0),
    )(*args)


def local(volumes, first_filter, second_filter, upstream_grad):
    slab = volumes.reshape(4, 32, 4096)
    first = first_filter.reshape(9, 192, 128)
    second = second_filter.reshape(27, 128, 128)
    upstream = upstream_grad.reshape(8, 16, 128)
    y_plane = (3, 33, 16, 128)
    w_scratch = ((2304, 128), BF16)

    rim = next_in_space(slab[3], 1)
    y, hidden_up = call(
        upper_plane_kernel,
        [((4,) + y_plane, BF16), ((512, 128), BF16)],
        slab, first, scratch=[w_scratch], flops=6 * 10**8,
    )
    hidden_rim = next_in_space(hidden_up, 1)
    y_rim, hidden_low = call(
        lower_plane_kernel,
        [(y_plane, BF16), ((512, 128), BF16)],
        rim, y, first, scratch=[w_scratch], flops=6 * 10**8,
    )
    second_out, grad_two, taps = call(
        second_conv_kernel,
        [((8, 16, 128), BF16), ((128, 128), BF16), ((128, SECOND_LANES), BF16)],
        hidden_rim, hidden_low, hidden_up, second.reshape(SECOND_LANES, 128), upstream,
        scratch=[((3, 17, 2, 24, 128), F32), ((128, 128), F32), ((128, 128), F32)],
        flops=2 * 10**8,
    )
    grad_two_next = next_in_space(grad_two, -1)
    keep, send = call(
        second_grad_kernel,
        [((64, SECOND_LANES), F32), ((64, SECOND_LANES), BF16)],
        taps, grad_two, scratch=[((128, SECOND_LANES), F32)], flops=4 * 10**8,
    )

    def over_core_and_x(keep, send):
        lanes = keep.shape[1]
        own, *pieces = call(
            after_core_kernel,
            [((16, lanes), F32)] + [((16, lanes), BF16)] * 3,
            keep, swap_core(send), scratch=[((64, lanes), F32)], flops=10**6,
        )
        return [own] + [ring_x(piece, k + 1) for k, piece in enumerate(pieces)]

    second_parts = over_core_and_x(keep, send)
    keep, send = call(
        first_grad_kernel,
        [((64, FIRST_LANES), F32), ((64, FIRST_LANES), BF16)],
        grad_two, grad_two_next, second, hidden_low, hidden_up, y_rim, y,
        scratch=[
            ((2, 17, 16, 128), F32), ((2, 16, 2, 16, 128), F32), ((128, FIRST_LANES), F32),
        ],
        flops=8 * 10**8,
    )
    first_parts = over_core_and_x(keep, send)
    lanes = FIRST_LANES + SECOND_LANES
    own, *pieces = call(
        after_x_kernel,
        [((4, lanes), F32)] + [((4, lanes), BF16)] * 3,
        *first_parts, *second_parts, scratch=[((4, 4, lanes), F32)], flops=10**6,
    )
    (total,) = call(
        after_z_kernel, [((4, lanes), BF16)],
        own, *[ring_z(piece, k + 1) for k, piece in enumerate(pieces)], flops=10**6,
    )
    (total,) = call(
        after_y_kernel, [((4, lanes), BF16)],
        total, *[ring_y(total, k) for k in (1, 2, 3)], flops=10**6,
    )
    first_grad, second_grad = call(
        final_kernel,
        [((27, 4, 64), F32), ((27, 4, 128), F32)],
        total, swap_z_low(total), flops=10**6,
    )
    return (
        second_out.reshape(1, 1, 8, 16, 128),
        jnp.swapaxes(first_grad, 1, 2).reshape(3, 3, 3, 64, 4),
        second_grad.reshape(3, 3, 3, 4, 128),
    )


def solution(mesh):
    placed = (P("dp", "space", None, None), P(), P(), P("dp", "space", None, None, None))
    return jax.shard_map(
        local,
        mesh=mesh,
        in_specs=placed,
        out_specs=(
            P("dp", "space", None, None, None),
            P(None, None, None, None, "space"),
            P(None, None, None, "space", None),
        ),
        check_vma=False,
    )
```

```python
import functools

import jax
import jax.numpy as jnp
from jax import lax
from jax.experimental import pallas as pl
from jax.experimental.pallas import tpu as pltpu
from jax.sharding import PartitionSpec as P

SLOPE = 0.3
F32, BF16 = jnp.float32, jnp.bfloat16
FIRST, SECOND = 14, 27


def around_space(value, by):
    return lax.ppermute(value, "space", [(i, (i + by) % 32) for i in range(32)])


def swap(value, axis, bit):
    size = {"space": 32, "dp": 8}[axis]
    return lax.ppermute(value, axis, [(i, i ^ bit) for i in range(size)])


CORE, X_ONE, X_TWO, Z_ONE, Z_TWO = 1, 8, 24, 2, 6
Y_ONE, Y_TWO, Z_LOW = 1, 3, 4


def leaky(values):
    return jnp.where(values > 0, values, SLOPE * values)


def dot(a, b):
    return jnp.dot(a, b, preferred_element_type=F32)


def dot_nt(a, b):
    return lax.dot_general(a, b, (((1,), (1,)), ((), ())), preferred_element_type=F32)


def rows_by_tap(keep=None):
    m = lax.broadcasted_iota(jnp.int32, (48, 32), 0)
    h = lax.broadcasted_iota(jnp.int32, (48, 32), 1)
    picked = h == 2 * (m & 15) + (m >> 4) - 1
    if keep is not None:
        picked = jnp.logical_and(picked, keep)
    return jnp.where(picked, 1.0, 0.0).astype(BF16)


def channel_order():
    s = lax.axis_index("space")
    m = lax.broadcasted_iota(jnp.int32, (128, 128), 0)
    i = lax.broadcasted_iota(jnp.int32, (128, 128), 1)
    core = (m >> 6) ^ (s & 1)
    x = ((m >> 5) & 1) ^ (3 * ((m >> 4) & 1)) ^ (s >> 3)
    z = ((m >> 3) & 1) ^ (3 * ((m >> 2) & 1)) ^ ((s >> 1) & 3)
    return jnp.where(i == x * 32 + z * 8 + core * 4 + (m & 3), 1.0, 0.0).astype(BF16)


def spread_rows(plane_ref, pick, y_ref):
    for t in range(3):
        y_ref[t, 0] = jnp.zeros((16, 128), BF16)
    for n in range(8):
        out = dot(pick, plane_ref[:, n * 512 : (n + 1) * 512]).astype(BF16)
        for t in range(3):
            for r in range(4):
                y_ref[t, 1 + 4 * n + r] = out[16 * t : 16 * t + 16, 128 * r : 128 * r + 128]


def columns(y_ref, b):
    before = y_ref[b, 0:32].reshape(512, 128)
    at = y_ref[b, 1:33].reshape(512, 128)
    return jnp.concatenate([before, at], axis=1)


def first_conv(planes, f_ref, w_ref):
    for ab in range(9):
        w_ref[ab * 256 : ab * 256 + 64] = jnp.zeros((64, 128), BF16)
        w_ref[ab * 256 + 64 : ab * 256 + 256] = f_ref[ab]
    lhs = jnp.concatenate([columns(planes[a], b) for a in range(3) for b in range(3)], axis=1)
    return leaky(dot(lhs, w_ref[...])).astype(BF16)


def rim_kernel(v_ref, rim_ref, sems):
    copies = [
        pltpu.make_async_copy(
            v_ref.at[3, 8 * k : 8 * k + 8], rim_ref.at[8 * k : 8 * k + 8], sems.at[k]
        )
        for k in range(4)
    ]
    for copy in copies:
        copy.start()
    for copy in copies:
        copy.wait()


def upper_plane_kernel(v_ref, f_ref, y_ref, hid_ref, v, f, w_ref, sems):
    copies = [pltpu.make_async_copy(v_ref.at[p + 1], v.at[p], sems.at[p]) for p in range(3)]
    copies.append(pltpu.make_async_copy(f_ref, f, sems.at[3]))
    for copy in copies:
        copy.start()
    pick = rows_by_tap()
    for p in range(3):
        copies[p].wait()
        spread_rows(v.at[p], pick, y_ref.at[p])
    copies[3].wait()
    hid_ref[...] = first_conv([y_ref.at[p] for p in range(3)], f, w_ref)


def lower_plane_kernel(rim_ref, v_ref, y_ref, f_ref, yl_ref, hid_ref, v, w_ref, sems):
    copy = pltpu.make_async_copy(v_ref.at[0], v, sems.at[0])
    copy.start()
    copy.wait()
    spread_rows(v, rows_by_tap(), yl_ref.at[1])
    spread_rows(rim_ref, rows_by_tap(lax.axis_index("space") > 0), yl_ref.at[0])
    hid_ref[...] = first_conv([yl_ref.at[0], yl_ref.at[1], y_ref.at[0]], f_ref, w_ref)


def second_conv_kernel(hm_ref, h0_ref, h1_ref, f_ref, up_ref, out_ref, gp_ref, t_ref, hs, us, os):
    inside = jnp.where(lax.axis_index("space") > 0, 1.0, 0.0)
    for a, h_ref in enumerate((hm_ref, h0_ref, h1_ref)):
        h = h_ref[...].astype(F32).reshape(16, 2, 16, 128)
        if a == 0:
            h = h * inside
        hs[a, :, :, 0:8, :] = jnp.zeros((17, 2, 8, 128), F32)
        hs[a, 0, 0] = jnp.zeros((24, 128), F32)
        hs[a, 0:16, 1, 8:24, :] = h[:, 0]
        hs[a, 1:17, 0, 8:24, :] = h[:, 1]
    taps = []
    for a in range(3):
        for b in range(3):
            for c in range(3):
                rows = hs[a, c // 2 : c // 2 + 16, c % 2, pl.ds(7 + b, 8, stride=2), :]
                taps.append(rows.reshape(128, 128).astype(BF16))
                t_ref[len(taps) * 128 - 128 : len(taps) * 128] = taps[-1]
    pre = dot(jnp.concatenate(taps, axis=1), f_ref[...])
    us[...] = up_ref[...].astype(F32).reshape(128, 128)
    up = jnp.concatenate([us[pl.ds(r, 8, stride=16), :] for r in range(16)], axis=0)
    gp_ref[...] = (up * jnp.where(pre > 0, 1.0, SLOPE)).astype(BF16)
    out = leaky(pre)
    for r in range(16):
        os[pl.ds(r, 8, stride=16), :] = out[8 * r : 8 * r + 8]
    out_ref[...] = os[...].astype(BF16).reshape(8, 16, 128)


def second_grad_kernel(t_ref, gp_ref, keep_ref, send_ref):
    turned = dot_nt(channel_order(), t_ref[...]).astype(BF16)
    gp = gp_ref[...]
    for start in range(0, SECOND, 9):
        lhs = [turned[:, tap * 128 : tap * 128 + 128] for tap in range(start, start + 9)]
        grad = dot(jnp.concatenate(lhs, axis=0), gp).reshape(9, 128, 128)
        keep_ref[start : start + 9] = grad[:, :64]
        send_ref[start : start + 9] = grad[:, 64:].astype(BF16)


def first_grad_kernel(
    gp_ref, gpn_ref, f_ref, h0_ref, h1_ref, yl_ref, y_ref, keep_ref, send_ref, gs, gu
):
    inside = jnp.where(lax.axis_index("space") < 31, 1.0, 0.0)
    gs[...] = jnp.zeros_like(gs)
    gs[0, 0:16, 0:8, :] = gp_ref[...].astype(F32).reshape(16, 8, 128)
    gs[1, 0:16, 0:8, :] = gpn_ref[...].astype(F32).reshape(16, 8, 128) * inside
    moved = {
        (s, dr, dq): gs[s, dr : dr + 16, dq : dq + 8, :].reshape(128, 128).astype(BF16)
        for s in range(2)
        for dr in range(2)
        for dq in range(2)
    }
    one_d = {0: [(0, 1)], 1: [(0, 2), (1, 0)]}
    for pu in range(2):
        for pv in range(2):
            for pw in range(2):
                lhs, rhs = [], []
                for s, a in one_d[pu]:
                    for dq, b in one_d[pv]:
                        for dr, c in one_d[pw]:
                            lhs.append(moved[s, dr, dq])
                            rhs.append(f_ref[9 * a + 3 * b + c])
                grad = dot_nt(jnp.concatenate(lhs, axis=1), jnp.concatenate(rhs, axis=1))
                grad = grad.astype(BF16).astype(F32).reshape(16, 8, 128)
                gu[pu, :, pw, pl.ds(pv, 8, stride=2), :] = grad
    grads = []
    for pu, h_ref in enumerate((h0_ref, h1_ref)):
        hid = h_ref[...].astype(F32)
        grads.append((gu[pu].reshape(512, 128) * jnp.where(hid > 0, 1.0, SLOPE)).astype(BF16))
    turned = dot_nt(channel_order(), jnp.concatenate(grads, axis=0)).astype(BF16)
    planes = [yl_ref.at[0], yl_ref.at[1]] + [y_ref.at[p] for p in range(3)]
    low = lax.broadcasted_iota(jnp.int32, (128, 128), 1) < 64

    def put(block, grad):
        keep_ref[block] = grad[:64]
        send_ref[block] = grad[64:].astype(BF16)

    held = None
    for a in range(3):
        for b in range(3):
            ab = 3 * a + b
            rhs = jnp.concatenate([columns(planes[a], b), columns(planes[a + 2], b)], axis=0)
            grad = dot(turned, rhs)
            put(ab, grad[:, 128:])
            if ab % 2 == 0:
                held = pltpu.roll(grad[:, :128], 64, axis=1)
            if ab % 2 == 1 or ab == 8:
                upper = grad[:, :128] if ab % 2 else jnp.zeros_like(held)
                put(9 + ab // 2, jnp.where(low, held, upper))


def fold_kernel(groups, *refs):
    count = 2 * sum(groups)
    ins, outs = list(refs[:count]), list(refs[count:])
    for parts in groups:
        keep_ref, send_ref = outs.pop(0), outs.pop(0)
        at = 0
        for _ in range(parts):
            own_ref, got_ref = ins.pop(0), ins.pop(0)
            total = own_ref[...] + got_ref[...].astype(F32)
            blocks, rows, _ = total.shape
            keep_ref[at : at + blocks] = total[:, : rows // 2]
            send_ref[at : at + blocks] = total[:, rows // 2 :].astype(BF16)
            at += blocks


def sum_kernel(*refs):
    *ins, out_ref = refs
    at = 0
    for own_ref, got_ref in zip(ins[::2], ins[1::2]):
        total = own_ref[...].astype(F32) + got_ref[...].astype(F32)
        out_ref[at : at + total.shape[0]] = total.astype(BF16)
        at += total.shape[0]


def final_kernel(own_ref, got_ref, first_ref, second_ref):
    total = own_ref[...].astype(F32) + got_ref[...].astype(F32)
    for ab in range(9):
        first_ref[3 * ab + 1] = total[ab, :, :64]
        first_ref[3 * ab + 2] = total[ab, :, 64:]
        at = (ab % 2) * 64
        first_ref[3 * ab] = total[9 + ab // 2, :, at : at + 64]
    second_ref[...] = total[FIRST:]


VMEM, HBM = pltpu.VMEM, pltpu.HBM


def call(kernel, outs, *args, scratch=(), spaces=None, flops=10**6, vmem=24 << 20):
    size = sum(a.size * a.dtype.itemsize for a in args)
    spaces = spaces or [VMEM] * len(args)
    return pl.pallas_call(
        kernel,
        out_shape=[jax.ShapeDtypeStruct(shape, dtype) for shape, dtype in outs],
        in_specs=[pl.BlockSpec(memory_space=space) for space in spaces],
        out_specs=[pl.BlockSpec(memory_space=VMEM)] * len(outs),
        scratch_shapes=[pltpu.VMEM(*s) if isinstance(s, tuple) else s for s in scratch],
        compiler_params=pltpu.CompilerParams(vmem_limit_bytes=vmem),
        cost_estimate=pl.CostEstimate(flops=flops, bytes_accessed=size, transcendentals=0),
    )(*args)


def fold(*groups):
    outs, args = [], []
    for group in groups:
        blocks = sum(own.shape[0] for own, _ in group)
        half = (blocks, group[0][0].shape[1] // 2, 128)
        outs += [(half, F32), (half, BF16)]
        args += [array for pair in group for array in pair]
    kernel = functools.partial(fold_kernel, [len(group) for group in groups])
    done = call(kernel, outs, *args)
    return list(zip(done[::2], done[1::2]))


def local(volumes, first_filter, second_filter, upstream_grad):
    slab = volumes.reshape(4, 32, 4096)
    first = first_filter.reshape(9, 192, 128)
    second = second_filter.reshape(27, 128, 128)
    upstream = upstream_grad.reshape(8, 16, 128)
    y_plane = (3, 33, 16, 128)
    w_scratch = ((2304, 128), BF16)
    dma = pltpu.SemaphoreType.DMA((4,))

    (rim,) = call(rim_kernel, [((32, 4096), BF16)], slab, spaces=[HBM], scratch=[dma], vmem=60 << 20)
    rim = around_space(rim, 1)
    y, hidden_up = call(
        upper_plane_kernel,
        [((3,) + y_plane, BF16), ((512, 128), BF16)],
        slab, first, spaces=[HBM, HBM],
        scratch=[((3, 32, 4096), BF16), ((9, 192, 128), BF16), w_scratch, dma], flops=6 * 10**8,
    )
    hidden_rim = around_space(hidden_up, 1)
    y_low, hidden_low = call(
        lower_plane_kernel,
        [((2,) + y_plane, BF16), ((512, 128), BF16)],
        rim, slab, y, first, spaces=[VMEM, HBM, VMEM, VMEM],
        scratch=[((32, 4096), BF16), w_scratch, dma], flops=6 * 10**8,
    )
    second_out, grad_two, taps = call(
        second_conv_kernel,
        [((8, 16, 128), BF16), ((128, 128), BF16), ((SECOND * 128, 128), BF16)],
        hidden_rim, hidden_low, hidden_up, second.reshape(SECOND * 128, 128), upstream,
        scratch=[((3, 17, 2, 24, 128), F32), ((128, 128), F32), ((128, 128), F32)],
        flops=2 * 10**8,
    )
    grad_two_next = around_space(grad_two, -1)
    keep2, send2 = call(
        second_grad_kernel,
        [((SECOND, 64, 128), F32), ((SECOND, 64, 128), BF16)],
        taps, grad_two, flops=4 * 10**8,
    )
    send2, grad_two_next = lax.optimization_barrier((send2, grad_two_next))
    keep1, send1 = call(
        first_grad_kernel,
        [((FIRST, 64, 128), F32), ((FIRST, 64, 128), BF16)],
        grad_two, grad_two_next, second, hidden_low, hidden_up, y_low, y,
        scratch=[((2, 17, 16, 128), F32), ((2, 16, 2, 16, 128), F32)], flops=8 * 10**8,
    )
    s = "space"
    got2, got1 = swap(send2, s, CORE), swap(send1, s, CORE)
    ((keep, send),) = fold([(keep1, got1), (keep2, got2)])
    for bit in (X_ONE, X_TWO, Z_ONE):
        ((keep, send),) = fold([(keep, swap(send, s, bit))])
    total = ((FIRST + SECOND, 4, 128), BF16)
    (both,) = call(sum_kernel, [total], keep, swap(send, s, Z_TWO))
    (both,) = call(sum_kernel, [total], both, swap(both, "dp", Y_ONE))
    (both,) = call(sum_kernel, [total], both, swap(both, "dp", Y_TWO))
    first_grad, second_grad = call(
        final_kernel,
        [((27, 4, 64), F32), ((27, 4, 128), F32)],
        both, swap(both, "dp", Z_LOW),
    )
    return (
        second_out.reshape(1, 1, 8, 16, 128),
        jnp.swapaxes(first_grad, 1, 2).reshape(3, 3, 3, 64, 4),
        second_grad.reshape(3, 3, 3, 4, 128),
    )


def solution(mesh):
    placed = (P("dp", "space", None, None), P(), P(), P("dp", "space", None, None, None))
    return jax.shard_map(
        local,
        mesh=mesh,
        in_specs=placed,
        out_specs=(
            P("dp", "space", None, None, None),
            P(None, None, None, None, "space"),
            P(None, None, None, "space", None),
        ),
        check_vma=False,
    )
```

```python
import functools

import jax
import jax.numpy as jnp
from jax import lax
from jax.experimental import pallas as pl
from jax.experimental.pallas import tpu as pltpu
from jax.sharding import PartitionSpec as P

SLOPE = 0.3
F32, BF16 = jnp.float32, jnp.bfloat16
FIRST, SECOND = 14, 27


def around_space(value, by):
    return lax.ppermute(value, "space", [(i, (i + by) % 32) for i in range(32)])


def swap(value, axis, bit):
    size = {"space": 32, "dp": 8}[axis]
    return lax.ppermute(value, axis, [(i, i ^ bit) for i in range(size)])


CORE, X_ONE, X_TWO, Z_ONE, Z_TWO = 1, 8, 24, 2, 6
Y_ONE, Y_TWO, Z_LOW = 1, 3, 4


def leaky(values):
    return jnp.where(values > 0, values, SLOPE * values)


def dot(a, b):
    return jnp.dot(a, b, preferred_element_type=F32)


def dot_nt(a, b):
    return lax.dot_general(a, b, (((1,), (1,)), ((), ())), preferred_element_type=F32)


def rows_by_tap(keep=None):
    m = lax.broadcasted_iota(jnp.int32, (48, 32), 0)
    h = lax.broadcasted_iota(jnp.int32, (48, 32), 1)
    picked = h == 2 * (m & 15) + (m >> 4) - 1
    if keep is not None:
        picked = jnp.logical_and(picked, keep)
    return jnp.where(picked, 1.0, 0.0).astype(BF16)


def channel_order(near, far):
    s = lax.axis_index("space")
    m = lax.broadcasted_iota(jnp.int32, (128, 128), 0)
    i = lax.broadcasted_iota(jnp.int32, (128, 128), 1)
    core = (m >> 6) ^ (s & 1)
    x = (near * ((m >> 5) & 1)) ^ (far * ((m >> 4) & 1)) ^ (s >> 3)
    z = ((m >> 3) & 1) ^ (3 * ((m >> 2) & 1)) ^ ((s >> 1) & 3)
    return jnp.where(i == x * 32 + z * 8 + core * 4 + (m & 3), 1.0, 0.0).astype(BF16)


def spread_rows(plane_ref, pick, y_ref):
    for t in range(3):
        y_ref[t, 0] = jnp.zeros((16, 128), BF16)
    for n in range(8):
        out = dot(pick, plane_ref[:, n * 512 : (n + 1) * 512]).astype(BF16)
        for t in range(3):
            for r in range(4):
                y_ref[t, 1 + 4 * n + r] = out[16 * t : 16 * t + 16, 128 * r : 128 * r + 128]


def columns(y_ref, b):
    before = y_ref[b, 0:32].reshape(512, 128)
    at = y_ref[b, 1:33].reshape(512, 128)
    return jnp.concatenate([before, at], axis=1)


def first_conv(planes, w):
    lhs = jnp.concatenate([columns(plane, b) for plane in planes for b in range(3)], axis=1)
    return dot(lhs, w)


def second_taps(hidden, hs):
    h = hidden.astype(F32).reshape(16, 2, 16, 128)
    hs[:, :, 0:8, :] = jnp.zeros((17, 2, 8, 128), F32)
    hs[0, 0] = jnp.zeros((24, 128), F32)
    hs[0:16, 1, 8:24, :] = h[:, 0]
    hs[1:17, 0, 8:24, :] = h[:, 1]
    taps = []
    for b in range(3):
        for c in range(3):
            rows = hs[c // 2 : c // 2 + 16, c % 2, pl.ds(7 + b, 8, stride=2), :]
            taps.append(rows.reshape(128, 128).astype(BF16))
    return taps


def upper_plane_kernel(
    v_ref, rim_ref, f_ref, f2_ref,
    y_ref, w_ref, f2a_ref, hid_ref, taps_ref, next_ref,
    v, f, hs, sems,
):
    copies = [
        pltpu.make_async_copy(v_ref.at[1], v.at[0], sems.at[0]),
        pltpu.make_async_copy(v_ref.at[2], v.at[1], sems.at[1]),
        pltpu.make_async_copy(f_ref, f, sems.at[2]),
        pltpu.make_async_copy(f2_ref.at[0:9], f2a_ref, sems.at[3]),
    ]
    for copy in copies:
        copy.start()
    pick = rows_by_tap()
    spread_rows(rim_ref, pick, y_ref.at[2])
    for p in range(2):
        copies[p].wait()
        spread_rows(v.at[p], pick, y_ref.at[p])
    copies[2].wait()
    for ab in range(9):
        w_ref[ab * 256 : ab * 256 + 64] = jnp.zeros((64, 128), BF16)
        w_ref[ab * 256 + 64 : ab * 256 + 256] = f[ab]
    hidden = leaky(first_conv([y_ref.at[p] for p in range(3)], w_ref[...])).astype(BF16)
    hid_ref[...] = hidden
    taps = second_taps(hidden, hs)
    for n, tap in enumerate(taps):
        taps_ref[n * 128 : n * 128 + 128] = tap
    copies[3].wait()
    next_ref[...] = dot(jnp.concatenate(taps, axis=1), f2a_ref[...].reshape(1152, 128))


def ahead_kernel(
    v_ref, y_ref, w_ref, f2_ref, taps_ref, y0_ref, f2b_ref, acc_ref, own_ref, v, sems
):
    copies = [
        pltpu.make_async_copy(v_ref.at[0], v, sems.at[0]),
        pltpu.make_async_copy(f2_ref.at[9:27], f2b_ref, sems.at[1]),
    ]
    for copy in copies:
        copy.start()
    copies[0].wait()
    spread_rows(v, rows_by_tap(), y0_ref)
    acc_ref[...] = first_conv([y0_ref, y_ref.at[0]], w_ref[768:])
    copies[1].wait()
    own = None
    for n in range(9):
        part = dot(taps_ref[n * 128 : n * 128 + 128], f2b_ref[9 + n])
        own = part if own is None else own + part
    own_ref[...] = own


def lower_plane_kernel(
    rim_ref, got_ref, w_ref, f2b_ref, acc_ref, own_ref, up_ref,
    yr_ref, hid_ref, taps_ref, out_ref, gp_ref,
    hs, us, os,
):
    inside = lax.axis_index("space") > 0
    spread_rows(rim_ref, rows_by_tap(inside), yr_ref)
    hidden = leaky(first_conv([yr_ref], w_ref[0:768]) + acc_ref[...]).astype(BF16)
    hid_ref[...] = hidden
    taps = second_taps(hidden, hs)
    for n, tap in enumerate(taps):
        taps_ref[n * 128 : n * 128 + 128] = tap
    pre = dot(jnp.concatenate(taps, axis=1), f2b_ref[0:9].reshape(1152, 128))
    pre = pre + own_ref[...] + got_ref[...] * jnp.where(inside, 1.0, 0.0)
    us[...] = up_ref[...].astype(F32).reshape(128, 128)
    up = jnp.concatenate([us[pl.ds(r, 8, stride=16), :] for r in range(16)], axis=0)
    gp_ref[...] = (up * jnp.where(pre > 0, 1.0, SLOPE)).astype(BF16)
    out = leaky(pre)
    for r in range(16):
        os[pl.ds(r, 8, stride=16), :] = out[8 * r : 8 * r + 8]
    out_ref[...] = os[...].astype(BF16).reshape(8, 16, 128)


def second_grad(order, taps_ref, gp):
    turned = dot_nt(order, taps_ref[...]).astype(BF16)
    lhs = [turned[:, tap * 128 : tap * 128 + 128] for tap in range(9)]
    return dot(jnp.concatenate(lhs, axis=0), gp).reshape(9, 128, 128)


def second_grad_kernel(low_ref, up_ref, gp_ref, keep_ref, send_ref):
    for n, taps_ref in enumerate((low_ref, up_ref)):
        grad = second_grad(channel_order(1, 3), taps_ref, gp_ref[...])
        keep_ref[9 * n : 9 * n + 9] = grad[:, :64]
        send_ref[9 * n : 9 * n + 9] = grad[:, 64:].astype(BF16)


def first_grad_kernel(
    gp_ref, gpn_ref, fa_ref, fb_ref, h0_ref, h1_ref, yr_ref, y0_ref, y_ref, taps_ref,
    keep_ref, send_ref, gs, gu,
):
    inside = jnp.where(lax.axis_index("space") < 31, 1.0, 0.0)
    gs[...] = jnp.zeros_like(gs)
    gs[0, 0:16, 0:8, :] = gp_ref[...].astype(F32).reshape(16, 8, 128)
    above = gpn_ref[...].astype(F32) * inside
    gs[1, 0:16, 0:8, :] = above.reshape(16, 8, 128)
    moved = {
        (s, dr, dq): gs[s, dr : dr + 16, dq : dq + 8, :].reshape(128, 128).astype(BF16)
        for s in range(2)
        for dr in range(2)
        for dq in range(2)
    }
    one_d = {0: [(0, 1)], 1: [(0, 2), (1, 0)]}
    for pu in range(2):
        for pv in range(2):
            for pw in range(2):
                lhs, rhs = [], []
                for s, a in one_d[pu]:
                    for dq, b in one_d[pv]:
                        for dr, c in one_d[pw]:
                            lhs.append(moved[s, dr, dq])
                            tap = 9 * a + 3 * b + c
                            rhs.append(fb_ref[tap - 9] if a else fa_ref[tap])
                grad = dot_nt(jnp.concatenate(lhs, axis=1), jnp.concatenate(rhs, axis=1))
                grad = grad.astype(BF16).astype(F32).reshape(16, 8, 128)
                gu[pu, :, pw, pl.ds(pv, 8, stride=2), :] = grad
    grads = []
    for pu, h_ref in enumerate((h0_ref, h1_ref)):
        hid = h_ref[...].astype(F32)
        grads.append((gu[pu].reshape(512, 128) * jnp.where(hid > 0, 1.0, SLOPE)).astype(BF16))
    order = channel_order(3, 1)
    turned = dot_nt(order, jnp.concatenate(grads, axis=0)).astype(BF16)
    planes = [yr_ref, y0_ref] + [y_ref.at[p] for p in range(3)]
    low = lax.broadcasted_iota(jnp.int32, (128, 128), 1) < 64

    def put(block, grad):
        keep_ref[block] = grad[:64]
        send_ref[block] = grad[64:].astype(BF16)

    held = None
    for a in range(3):
        for b in range(3):
            ab = 3 * a + b
            rhs = jnp.concatenate([columns(planes[a], b), columns(planes[a + 2], b)], axis=0)
            grad = dot(turned, rhs)
            put(ab, grad[:, 128:])
            if ab % 2 == 0:
                held = pltpu.roll(grad[:, :128], 64, axis=1)
            if ab % 2 == 1 or ab == 8:
                upper = grad[:, :128] if ab % 2 else jnp.zeros_like(held)
                put(9 + ab // 2, jnp.where(low, held, upper))
    grad = second_grad(order, taps_ref, above.astype(BF16))
    keep_ref[FIRST:] = grad[:, :64]
    send_ref[FIRST:] = grad[:, 64:].astype(BF16)


def fold_kernel(groups, *refs):
    count = 2 * sum(groups)
    ins, outs = list(refs[:count]), list(refs[count:])
    for parts in groups:
        keep_ref, send_ref = outs.pop(0), outs.pop(0)
        at = 0
        for _ in range(parts):
            own_ref, got_ref = ins.pop(0), ins.pop(0)
            total = own_ref[...] + got_ref[...].astype(F32)
            blocks, rows, _ = total.shape
            keep_ref[at : at + blocks] = total[:, : rows // 2]
            send_ref[at : at + blocks] = total[:, rows // 2 :].astype(BF16)
            at += blocks


def sum_kernel(*refs):
    *ins, out_ref = refs
    at = 0
    for own_ref, got_ref in zip(ins[::2], ins[1::2]):
        total = own_ref[...].astype(F32) + got_ref[...].astype(F32)
        out_ref[at : at + total.shape[0]] = total.astype(BF16)
        at += total.shape[0]


def final_kernel(own_ref, got_ref, first_ref, second_ref):
    total = own_ref[...].astype(F32) + got_ref[...].astype(F32)
    for ab in range(9):
        first_ref[3 * ab + 1] = total[18 + ab, :, :64]
        first_ref[3 * ab + 2] = total[18 + ab, :, 64:]
        at = (ab % 2) * 64
        first_ref[3 * ab] = total[27 + ab // 2, :, at : at + 64]
    second_ref[9:27] = total[:18]
    second_ref[0:9] = total[18 + FIRST :]


VMEM, HBM = pltpu.VMEM, pltpu.HBM


def call(kernel, outs, *args, scratch=(), spaces=None, flops=10**6):
    size = sum(a.size * a.dtype.itemsize for a in args)
    spaces = spaces or [VMEM] * len(args)
    return pl.pallas_call(
        kernel,
        out_shape=[jax.ShapeDtypeStruct(shape, dtype) for shape, dtype in outs],
        in_specs=[pl.BlockSpec(memory_space=space) for space in spaces],
        out_specs=[pl.BlockSpec(memory_space=VMEM)] * len(outs),
        scratch_shapes=[pltpu.VMEM(*s) if isinstance(s, tuple) else s for s in scratch],
        compiler_params=pltpu.CompilerParams(vmem_limit_bytes=24 << 20),
        cost_estimate=pl.CostEstimate(flops=flops, bytes_accessed=size, transcendentals=0),
    )(*args)


def in_hbm(value):
    return pltpu.with_memory_space_constraint(value, HBM)


def fold(*groups):
    outs, args = [], []
    for group in groups:
        blocks = sum(own.shape[0] for own, _ in group)
        half = (blocks, group[0][0].shape[1] // 2, 128)
        outs += [(half, F32), (half, BF16)]
        args += [array for pair in group for array in pair]
    kernel = functools.partial(fold_kernel, [len(group) for group in groups])
    done = call(kernel, outs, *args)
    return list(zip(done[::2], done[1::2]))


def local(volumes, first_filter, second_filter, upstream_grad):
    slab = in_hbm(volumes.reshape(4, 32, 4096))
    first = in_hbm(first_filter.reshape(9, 192, 128))
    second = in_hbm(second_filter.reshape(27, 128, 128))
    upstream = upstream_grad.reshape(8, 16, 128)
    y_plane = (3, 33, 16, 128)
    hs = ((17, 2, 24, 128), F32)
    tile = ((128, 128), F32)

    rim_up = volumes[0, 3]
    rim = around_space(rim_up, 1)
    y, w, second_a, hidden_up, taps_up, to_next = call(
        upper_plane_kernel,
        [
            ((3,) + y_plane, BF16), ((2304, 128), BF16), ((9, 128, 128), BF16),
            ((512, 128), BF16), ((1152, 128), BF16), tile,
        ],
        slab, rim_up, first, second, spaces=[HBM, VMEM, HBM, HBM],
        scratch=[((2, 32, 4096), BF16), ((9, 192, 128), BF16), hs, pltpu.SemaphoreType.DMA((4,))],
        flops=10**9,
    )
    from_below = around_space(to_next, 1)
    y_low, second_b, partial_low, from_up = call(
        ahead_kernel,
        [(y_plane, BF16), ((18, 128, 128), BF16), ((512, 128), F32), tile],
        slab, y, w, second, taps_up, spaces=[HBM, VMEM, VMEM, HBM, VMEM],
        scratch=[((32, 4096), BF16), pltpu.SemaphoreType.DMA((2,))], flops=10**9,
    )
    y_rim, hidden_low, taps_low, second_out, grad_two = call(
        lower_plane_kernel,
        [
            (y_plane, BF16), ((512, 128), BF16), ((1152, 128), BF16),
            ((8, 16, 128), BF16), ((128, 128), BF16),
        ],
        rim, from_below, w, second_b, partial_low, from_up, upstream,
        scratch=[hs, tile, tile], flops=4 * 10**8,
    )
    grad_two_next = around_space(grad_two, -1)
    keep2, send2 = call(
        second_grad_kernel,
        [((18, 64, 128), F32), ((18, 64, 128), BF16)],
        taps_low, taps_up, grad_two, flops=4 * 10**8,
    )
    send2, grad_two_next = lax.optimization_barrier((send2, grad_two_next))
    blocks = FIRST + 9
    keep1, send1 = call(
        first_grad_kernel,
        [((blocks, 64, 128), F32), ((blocks, 64, 128), BF16)],
        grad_two, grad_two_next, second_a, second_b, hidden_low, hidden_up,
        y_rim, y_low, y, taps_up,
        scratch=[((2, 17, 16, 128), F32), ((2, 16, 2, 16, 128), F32)], flops=8 * 10**8,
    )
    s = "space"
    got2, got1 = swap(send2, s, CORE), swap(send1, s, CORE)
    (keep2, send2), (keep1, send1) = fold([(keep2, got2)], [(keep1, got1)])
    got2, got1 = swap(send2, s, X_ONE), swap(send1, s, X_TWO)
    (keep2, send2), (keep1, send1) = fold([(keep2, got2)], [(keep1, got1)])
    got2, got1 = swap(send2, s, X_TWO), swap(send1, s, X_ONE)
    ((keep, send),) = fold([(keep2, got2), (keep1, got1)])
    ((keep, send),) = fold([(keep, swap(send, s, Z_ONE))])
    total = ((FIRST + SECOND, 4, 128), BF16)
    (both,) = call(sum_kernel, [total], keep, swap(send, s, Z_TWO))
    (both,) = call(sum_kernel, [total], both, swap(both, "dp", Y_ONE))
    (both,) = call(sum_kernel, [total], both, swap(both, "dp", Y_TWO))
    first_grad, second_grad = call(
        final_kernel,
        [((27, 4, 64), F32), ((27, 4, 128), F32)],
        both, swap(both, "dp", Z_LOW),
    )
    return (
        second_out.reshape(1, 1, 8, 16, 128),
        jnp.swapaxes(first_grad, 1, 2).reshape(3, 3, 3, 64, 4),
        second_grad.reshape(3, 3, 3, 4, 128),
    )


def solution(mesh):
    placed = (P("dp", "space", None, None), P(), P(), P("dp", "space", None, None, None))
    return jax.shard_map(
        local,
        mesh=mesh,
        in_specs=placed,
        out_specs=(
            P("dp", "space", None, None, None),
            P(None, None, None, None, "space"),
            P(None, None, None, "space", None),
        ),
        check_vma=False,
    )
```

```python
import jax
import jax.numpy as jnp
from jax import lax
from jax.experimental import pallas as pl
from jax.experimental.pallas import tpu as pltpu
from jax.sharding import PartitionSpec as P

SLOPE = 0.3
F32, BF16 = jnp.float32, jnp.bfloat16
FIRST, SECOND = 14, 27


def around_space(value, by):
    return lax.ppermute(value, "space", [(i, (i + by) % 32) for i in range(32)])


def swap_core(value):
    return lax.ppermute(value, "space", [(i, i ^ 1) for i in range(32)])


def partner(axis, step, core):
    near = 1 if (step + core) % 2 == 0 else 3
    return near << {"x": 3, "z": 1, "y": 0}[axis]


def swap(value, axis, step):
    if axis == "y":
        pairs = [
            (d * 32 + s, (d ^ partner(axis, step, s & 1)) * 32 + s) for d in range(8) for s in range(32)
        ]
        return lax.ppermute(value, ("dp", "space"), pairs)
    return lax.ppermute(value, "space", [(s, s ^ partner(axis, step, s & 1)) for s in range(32)])


def swap_z_low(value):
    return lax.ppermute(value, "dp", [(d, d ^ 4) for d in range(8)])


def leaky(values):
    return jnp.where(values > 0, values, SLOPE * values)


def dot(a, b):
    return jnp.dot(a, b, preferred_element_type=F32)


def dot_nt(a, b):
    return lax.dot_general(a, b, (((1,), (1,)), ((), ())), preferred_element_type=F32)


def rows_by_tap(keep=None):
    m = lax.broadcasted_iota(jnp.int32, (48, 32), 0)
    h = lax.broadcasted_iota(jnp.int32, (48, 32), 1)
    picked = h == 2 * (m & 15) + (m >> 4) - 1
    if keep is not None:
        picked = jnp.logical_and(picked, keep)
    return jnp.where(picked, 1.0, 0.0).astype(BF16)


def channel_order():
    s = lax.axis_index("space")
    m = lax.broadcasted_iota(jnp.int32, (128, 128), 0)
    i = lax.broadcasted_iota(jnp.int32, (128, 128), 1)
    core = (m >> 6) ^ (s & 1)
    near, far = 1 + 2 * core, 3 - 2 * core
    x = (near * ((m >> 5) & 1)) ^ (far * ((m >> 4) & 1)) ^ (s >> 3)
    z = (near * ((m >> 3) & 1)) ^ (far * ((m >> 2) & 1)) ^ ((s >> 1) & 3)
    return jnp.where(i == x * 32 + z * 8 + core * 4 + (m & 3), 1.0, 0.0).astype(BF16)


def spread_rows(plane_ref, pick, y_ref):
    for t in range(3):
        y_ref[t, 0] = jnp.zeros((16, 128), BF16)
    for n in range(8):
        out = dot(pick, plane_ref[:, n * 512 : (n + 1) * 512]).astype(BF16)
        for t in range(3):
            for r in range(4):
                y_ref[t, 1 + 4 * n + r] = out[16 * t : 16 * t + 16, 128 * r : 128 * r + 128]


def columns(y_ref, b):
    before = y_ref[b, 0:32].reshape(512, 128)
    at = y_ref[b, 1:33].reshape(512, 128)
    return jnp.concatenate([before, at], axis=1)


def first_conv(planes, w):
    lhs = jnp.concatenate([columns(plane, b) for plane in planes for b in range(3)], axis=1)
    return dot(lhs, w)


def second_taps(hidden, hs):
    h = hidden.astype(F32).reshape(16, 2, 16, 128)
    hs[:, :, 0:8, :] = jnp.zeros((17, 2, 8, 128), F32)
    hs[0, 0] = jnp.zeros((24, 128), F32)
    hs[0:16, 1, 8:24, :] = h[:, 0]
    hs[1:17, 0, 8:24, :] = h[:, 1]
    taps = []
    for b in range(3):
        for c in range(3):
            rows = hs[c // 2 : c // 2 + 16, c % 2, pl.ds(7 + b, 8, stride=2), :]
            taps.append(rows.reshape(128, 128).astype(BF16))
    return taps


def upper_plane_kernel(
    v_ref, rim_ref, f_ref, f2_ref,
    y_ref, w_ref, f2a_ref, hid_ref, taps_ref, next_ref,
    v, f, hs, sems,
):
    copies = [
        pltpu.make_async_copy(v_ref.at[1], v.at[0], sems.at[0]),
        pltpu.make_async_copy(v_ref.at[2], v.at[1], sems.at[1]),
        pltpu.make_async_copy(f_ref, f, sems.at[2]),
        pltpu.make_async_copy(f2_ref.at[0:9], f2a_ref, sems.at[3]),
    ]
    for copy in copies:
        copy.start()
    pick = rows_by_tap()
    spread_rows(rim_ref, pick, y_ref.at[2])
    for p in range(2):
        copies[p].wait()
        spread_rows(v.at[p], pick, y_ref.at[p])
    copies[2].wait()
    for ab in range(9):
        w_ref[ab * 256 : ab * 256 + 64] = jnp.zeros((64, 128), BF16)
        w_ref[ab * 256 + 64 : ab * 256 + 256] = f[ab]
    hidden = leaky(first_conv([y_ref.at[p] for p in range(3)], w_ref[...])).astype(BF16)
    hid_ref[...] = hidden
    taps = second_taps(hidden, hs)
    for n, tap in enumerate(taps):
        taps_ref[n * 128 : n * 128 + 128] = tap
    copies[3].wait()
    next_ref[...] = dot(jnp.concatenate(taps, axis=1), f2a_ref[...].reshape(1152, 128))


def ahead_kernel(
    v_ref, y_ref, w_ref, f2_ref, taps_ref, y0_ref, f2b_ref, acc_ref, own_ref, v, sems
):
    copies = [
        pltpu.make_async_copy(v_ref.at[0], v, sems.at[0]),
        pltpu.make_async_copy(f2_ref.at[9:27], f2b_ref, sems.at[1]),
    ]
    for copy in copies:
        copy.start()
    copies[0].wait()
    spread_rows(v, rows_by_tap(), y0_ref)
    acc_ref[...] = first_conv([y0_ref, y_ref.at[0]], w_ref[768:])
    copies[1].wait()
    own = None
    for n in range(9):
        part = dot(taps_ref[n * 128 : n * 128 + 128], f2b_ref[9 + n])
        own = part if own is None else own + part
    own_ref[...] = own


def lower_plane_kernel(
    rim_ref, got_ref, w_ref, f2b_ref, acc_ref, own_ref, up_ref,
    yr_ref, hid_ref, taps_ref, out_ref, gp_ref,
    hs, us,
):
    inside = lax.axis_index("space") > 0
    spread_rows(rim_ref, rows_by_tap(inside), yr_ref)
    hidden = leaky(first_conv([yr_ref], w_ref[0:768]) + acc_ref[...]).astype(BF16)
    hid_ref[...] = hidden
    taps = second_taps(hidden, hs)
    for n, tap in enumerate(taps):
        taps_ref[n * 128 : n * 128 + 128] = tap
    pre = dot(jnp.concatenate(taps, axis=1), f2b_ref[0:9].reshape(1152, 128))
    pre = pre + own_ref[...] + got_ref[...] * jnp.where(inside, 1.0, 0.0)
    us[...] = up_ref[...].astype(F32).reshape(128, 128)
    up = jnp.concatenate([us[pl.ds(r, 8, stride=16), :] for r in range(16)], axis=0)
    gp_ref[...] = (up * jnp.where(pre > 0, 1.0, SLOPE)).astype(BF16)
    out_ref[...] = leaky(pre)


def second_grad(order, taps_ref, gp):
    turned = dot_nt(order, taps_ref[...]).astype(BF16)
    lhs = [turned[:, tap * 128 : tap * 128 + 128] for tap in range(9)]
    return dot(jnp.concatenate(lhs, axis=0), gp).reshape(9, 128, 128)


def second_grad_kernel(low_ref, up_ref, gp_ref, pre_ref, keep_ref, send_ref, out_ref, os):
    order = channel_order()
    for n, taps_ref in enumerate((low_ref, up_ref)):
        grad = second_grad(order, taps_ref, gp_ref[...])
        keep_ref[9 * n : 9 * n + 9] = grad[:, :64]
        send_ref[9 * n : 9 * n + 9] = grad[:, 64:].astype(BF16)
    for r in range(16):
        os[pl.ds(r, 8, stride=16), :] = pre_ref[8 * r : 8 * r + 8]
    out_ref[...] = os[...].astype(BF16).reshape(8, 16, 128)


def first_grad_kernel(
    gp_ref, gpn_ref, fa_ref, fb_ref, h0_ref, h1_ref, yr_ref, y0_ref, y_ref, taps_ref,
    keep_ref, send_ref, gs, gu,
):
    inside = jnp.where(lax.axis_index("space") < 31, 1.0, 0.0)
    gs[...] = jnp.zeros_like(gs)
    gs[0, 0:16, 0:8, :] = gp_ref[...].astype(F32).reshape(16, 8, 128)
    above = gpn_ref[...].astype(F32) * inside
    gs[1, 0:16, 0:8, :] = above.reshape(16, 8, 128)
    moved = {
        (s, dr, dq): gs[s, dr : dr + 16, dq : dq + 8, :].reshape(128, 128).astype(BF16)
        for s in range(2)
        for dr in range(2)
        for dq in range(2)
    }
    one_d = {0: [(0, 1)], 1: [(0, 2), (1, 0)]}
    for pu in range(2):
        for pv in range(2):
            for pw in range(2):
                lhs, rhs = [], []
                for s, a in one_d[pu]:
                    for dq, b in one_d[pv]:
                        for dr, c in one_d[pw]:
                            lhs.append(moved[s, dr, dq])
                            tap = 9 * a + 3 * b + c
                            rhs.append(fb_ref[tap - 9] if a else fa_ref[tap])
                grad = dot_nt(jnp.concatenate(lhs, axis=1), jnp.concatenate(rhs, axis=1))
                grad = grad.astype(BF16).astype(F32).reshape(16, 8, 128)
                gu[pu, :, pw, pl.ds(pv, 8, stride=2), :] = grad
    grads = []
    for pu, h_ref in enumerate((h0_ref, h1_ref)):
        hid = h_ref[...].astype(F32)
        grads.append((gu[pu].reshape(512, 128) * jnp.where(hid > 0, 1.0, SLOPE)).astype(BF16))
    order = channel_order()
    turned = dot_nt(order, jnp.concatenate(grads, axis=0)).astype(BF16)
    planes = [yr_ref, y0_ref] + [y_ref.at[p] for p in range(3)]
    low = lax.broadcasted_iota(jnp.int32, (128, 128), 1) < 64

    def put(block, grad):
        keep_ref[block] = grad[:64]
        send_ref[block] = grad[64:].astype(BF16)

    held = None
    for a in range(3):
        for b in range(3):
            ab = 3 * a + b
            rhs = jnp.concatenate([columns(planes[a], b), columns(planes[a + 2], b)], axis=0)
            grad = dot(turned, rhs)
            put(ab, grad[:, 128:])
            if ab % 2 == 0:
                held = pltpu.roll(grad[:, :128], 64, axis=1)
            if ab % 2 == 1 or ab == 8:
                upper = grad[:, :128] if ab % 2 else jnp.zeros_like(held)
                put(9 + ab // 2, jnp.where(low, held, upper))
    grad = second_grad(order, taps_ref, above.astype(BF16))
    keep_ref[FIRST:] = grad[:, :64]
    send_ref[FIRST:] = grad[:, 64:].astype(BF16)


def fold_kernel(own_ref, got_ref, keep_ref, send_ref):
    total = own_ref[...] + got_ref[...].astype(F32)
    half = total.shape[1] // 2
    keep_ref[...] = total[:, :half]
    send_ref[...] = total[:, half:].astype(BF16)


def join_kernel(own_ref, got_ref, own2_ref, got2_ref, out_ref):
    out_ref[:18] = (own_ref[...] + got_ref[...].astype(F32)).astype(BF16)
    out_ref[18:] = (own2_ref[...] + got2_ref[...].astype(F32)).astype(BF16)


def sum_kernel(own_ref, got_ref, out_ref):
    out_ref[...] = (own_ref[...].astype(F32) + got_ref[...].astype(F32)).astype(BF16)


def final_kernel(own_ref, got_ref, first_ref, second_ref):
    total = own_ref[...].astype(F32) + got_ref[...].astype(F32)
    for ab in range(9):
        first_ref[3 * ab + 1] = total[18 + ab, :, :64]
        first_ref[3 * ab + 2] = total[18 + ab, :, 64:]
        at = (ab % 2) * 64
        first_ref[3 * ab] = total[27 + ab // 2, :, at : at + 64]
    second_ref[9:27] = total[:18]
    second_ref[0:9] = total[18 + FIRST :]


VMEM, HBM = pltpu.VMEM, pltpu.HBM


def call(kernel, outs, *args, scratch=(), spaces=None, flops=10**6):
    size = sum(a.size * a.dtype.itemsize for a in args)
    spaces = spaces or [VMEM] * len(args)
    return pl.pallas_call(
        kernel,
        out_shape=[jax.ShapeDtypeStruct(shape, dtype) for shape, dtype in outs],
        in_specs=[pl.BlockSpec(memory_space=space) for space in spaces],
        out_specs=[pl.BlockSpec(memory_space=VMEM)] * len(outs),
        scratch_shapes=[pltpu.VMEM(*s) if isinstance(s, tuple) else s for s in scratch],
        compiler_params=pltpu.CompilerParams(vmem_limit_bytes=24 << 20),
        cost_estimate=pl.CostEstimate(flops=flops, bytes_accessed=size, transcendentals=0),
    )(*args)


def in_hbm(value):
    return pltpu.with_memory_space_constraint(value, HBM)


def fold(own, got):
    half = (own.shape[0], own.shape[1] // 2, 128)
    return call(fold_kernel, [(half, F32), (half, BF16)], own, got)


def local(volumes, first_filter, second_filter, upstream_grad):
    slab = in_hbm(volumes.reshape(4, 32, 4096))
    first = in_hbm(first_filter.reshape(9, 192, 128))
    second = in_hbm(second_filter.reshape(27, 128, 128))
    upstream = upstream_grad.reshape(8, 16, 128)
    y_plane = (3, 33, 16, 128)
    hs = ((17, 2, 24, 128), F32)
    tile = ((128, 128), F32)

    rim_up = volumes[0, 3]
    rim = around_space(rim_up, 1)
    y, w, second_a, hidden_up, taps_up, to_next = call(
        upper_plane_kernel,
        [
            ((3,) + y_plane, BF16), ((2304, 128), BF16), ((9, 128, 128), BF16),
            ((512, 128), BF16), ((1152, 128), BF16), tile,
        ],
        slab, rim_up, first, second, spaces=[HBM, VMEM, HBM, HBM],
        scratch=[((2, 32, 4096), BF16), ((9, 192, 128), BF16), hs, pltpu.SemaphoreType.DMA((4,))],
        flops=10**9,
    )
    from_below = around_space(to_next, 1)
    y_low, second_b, partial_low, from_up = call(
        ahead_kernel,
        [(y_plane, BF16), ((18, 128, 128), BF16), ((512, 128), F32), tile],
        slab, y, w, second, taps_up, spaces=[HBM, VMEM, VMEM, HBM, VMEM],
        scratch=[((32, 4096), BF16), pltpu.SemaphoreType.DMA((2,))], flops=10**9,
    )
    y_rim, hidden_low, taps_low, out, grad_two = call(
        lower_plane_kernel,
        [
            (y_plane, BF16), ((512, 128), BF16), ((1152, 128), BF16),
            tile, ((128, 128), BF16),
        ],
        rim, from_below, w, second_b, partial_low, from_up, upstream,
        scratch=[hs, tile], flops=4 * 10**8,
    )
    grad_two_next = around_space(grad_two, -1)
    keep_a, send_a, second_out = call(
        second_grad_kernel,
        [((18, 64, 128), F32), ((18, 64, 128), BF16), ((8, 16, 128), BF16)],
        taps_low, taps_up, grad_two, out, scratch=[tile], flops=4 * 10**8,
    )
    send_a, grad_two_next = lax.optimization_barrier((send_a, grad_two_next))
    keep_b, send_b = call(
        first_grad_kernel,
        [((23, 64, 128), F32), ((23, 64, 128), BF16)],
        grad_two, grad_two_next, second_a, second_b, hidden_low, hidden_up,
        y_rim, y_low, y, taps_up,
        scratch=[((2, 17, 16, 128), F32), ((2, 16, 2, 16, 128), F32)], flops=8 * 10**8,
    )
    keep_a, send_a = fold(keep_a, swap_core(send_a))
    keep_b, send_b = fold(keep_b, swap_core(send_b))
    for axis, step in (("x", 0), ("x", 1), ("z", 0)):
        keep_a, send_a = fold(keep_a, swap(send_a, axis, step))
        keep_b, send_b = fold(keep_b, swap(send_b, axis, step))
    total = ((FIRST + SECOND, 4, 128), BF16)
    (both,) = call(
        join_kernel, [total], keep_a, swap(send_a, "z", 1), keep_b, swap(send_b, "z", 1)
    )
    (both,) = call(sum_kernel, [total], both, swap(both, "y", 0))
    (both,) = call(sum_kernel, [total], both, swap(both, "y", 1))
    first_grad, second_grad = call(
        final_kernel,
        [((27, 4, 64), F32), ((27, 4, 128), F32)],
        both, swap_z_low(both),
    )
    return (
        second_out.reshape(1, 1, 8, 16, 128),
        jnp.swapaxes(first_grad, 1, 2).reshape(3, 3, 3, 64, 4),
        second_grad.reshape(3, 3, 3, 4, 128),
    )


def solution(mesh):
    placed = (P("dp", "space", None, None), P(), P(), P("dp", "space", None, None, None))
    return jax.shard_map(
        local,
        mesh=mesh,
        in_specs=placed,
        out_specs=(
            P("dp", "space", None, None, None),
            P(None, None, None, None, "space"),
            P(None, None, None, "space", None),
        ),
        check_vma=False,
    )
```

```python
import functools

import jax
import jax.numpy as jnp
from jax import lax
from jax.experimental import pallas as pl
from jax.experimental.pallas import tpu as pltpu
from jax.sharding import PartitionSpec as P

SLOPE = 0.3
F32, BF16 = jnp.float32, jnp.bfloat16
FIRST, SECOND = 14, 27


def around_space(value, by):
    return lax.ppermute(value, "space", [(i, (i + by) % 32) for i in range(32)])


def swap_core(value):
    return lax.ppermute(value, "space", [(i, i ^ 1) for i in range(32)])


def partner(step, core):
    return 1 if (step + core) % 2 == 0 else 3


def swap_x(value, step):
    return lax.ppermute(value, "space", [(s, s ^ (partner(step, s & 1) << 3)) for s in range(32)])


def swap_z(value, slot):
    return lax.ppermute(value, "space", [(s, s ^ (slot << 1)) for s in range(32)])


def swap_y(value, slot):
    return lax.ppermute(value, "dp", [(d, d ^ slot) for d in range(8)])


def swap_z_low(value):
    return lax.ppermute(value, "dp", [(d, d ^ 4) for d in range(8)])


def leaky(values):
    return jnp.where(values > 0, values, SLOPE * values)


def dot(a, b):
    return jnp.dot(a, b, preferred_element_type=F32)


def dot_nt(a, b):
    return lax.dot_general(a, b, (((1,), (1,)), ((), ())), preferred_element_type=F32)


def rows_by_tap(keep=None):
    m = lax.broadcasted_iota(jnp.int32, (48, 32), 0)
    h = lax.broadcasted_iota(jnp.int32, (48, 32), 1)
    picked = h == 2 * (m & 15) + (m >> 4) - 1
    if keep is not None:
        picked = jnp.logical_and(picked, keep)
    return jnp.where(picked, 1.0, 0.0).astype(BF16)


def channel_order():
    s = lax.axis_index("space")
    m = lax.broadcasted_iota(jnp.int32, (128, 128), 0)
    i = lax.broadcasted_iota(jnp.int32, (128, 128), 1)
    core = (m >> 6) ^ (s & 1)
    near, far = 1 + 2 * core, 3 - 2 * core
    x = (near * ((m >> 5) & 1)) ^ (far * ((m >> 4) & 1)) ^ (s >> 3)
    z = ((m >> 2) & 3) ^ ((s >> 1) & 3)
    return jnp.where(i == x * 32 + z * 8 + core * 4 + (m & 3), 1.0, 0.0).astype(BF16)


def spread_rows(plane_ref, pick, y_ref):
    for t in range(3):
        y_ref[t, 0] = jnp.zeros((16, 128), BF16)
    for n in range(8):
        out = dot(pick, plane_ref[:, n * 512 : (n + 1) * 512]).astype(BF16)
        for t in range(3):
            for r in range(4):
                y_ref[t, 1 + 4 * n + r] = out[16 * t : 16 * t + 16, 128 * r : 128 * r + 128]


def columns(y_ref, b):
    before = y_ref[b, 0:32].reshape(512, 128)
    at = y_ref[b, 1:33].reshape(512, 128)
    return jnp.concatenate([before, at], axis=1)


def first_conv(planes, w):
    lhs = jnp.concatenate([columns(plane, b) for plane in planes for b in range(3)], axis=1)
    return dot(lhs, w)


def second_taps(hidden, hs):
    h = hidden.astype(F32).reshape(16, 2, 16, 128)
    hs[:, :, 0:8, :] = jnp.zeros((17, 2, 8, 128), F32)
    hs[0, 0] = jnp.zeros((24, 128), F32)
    hs[0:16, 1, 8:24, :] = h[:, 0]
    hs[1:17, 0, 8:24, :] = h[:, 1]
    taps = []
    for b in range(3):
        for c in range(3):
            rows = hs[c // 2 : c // 2 + 16, c % 2, pl.ds(7 + b, 8, stride=2), :]
            taps.append(rows.reshape(128, 128).astype(BF16))
    return taps


def upper_plane_kernel(
    v_ref, rim_ref, f_ref, f2_ref,
    y_ref, w_ref, f2a_ref, hid_ref, taps_ref, next_ref,
    v, f, hs, sems,
):
    copies = [
        pltpu.make_async_copy(v_ref.at[1], v.at[0], sems.at[0]),
        pltpu.make_async_copy(v_ref.at[2], v.at[1], sems.at[1]),
        pltpu.make_async_copy(f_ref, f, sems.at[2]),
        pltpu.make_async_copy(f2_ref.at[0:9], f2a_ref, sems.at[3]),
    ]
    for copy in copies:
        copy.start()
    pick = rows_by_tap()
    spread_rows(rim_ref, pick, y_ref.at[2])
    for p in range(2):
        copies[p].wait()
        spread_rows(v.at[p], pick, y_ref.at[p])
    copies[2].wait()
    for ab in range(9):
        w_ref[ab * 256 : ab * 256 + 64] = jnp.zeros((64, 128), BF16)
        w_ref[ab * 256 + 64 : ab * 256 + 256] = f[ab]
    hidden = leaky(first_conv([y_ref.at[p] for p in range(3)], w_ref[...])).astype(BF16)
    hid_ref[...] = hidden
    taps = second_taps(hidden, hs)
    for n, tap in enumerate(taps):
        taps_ref[n * 128 : n * 128 + 128] = tap
    copies[3].wait()
    next_ref[...] = dot(jnp.concatenate(taps, axis=1), f2a_ref[...].reshape(1152, 128))


def ahead_kernel(
    v_ref, y_ref, w_ref, f2_ref, taps_ref, y0_ref, f2b_ref, acc_ref, own_ref, v, sems
):
    copies = [
        pltpu.make_async_copy(v_ref.at[0], v, sems.at[0]),
        pltpu.make_async_copy(f2_ref.at[9:27], f2b_ref, sems.at[1]),
    ]
    for copy in copies:
        copy.start()
    copies[0].wait()
    spread_rows(v, rows_by_tap(), y0_ref)
    acc_ref[...] = first_conv([y0_ref, y_ref.at[0]], w_ref[768:])
    copies[1].wait()
    own = None
    for n in range(9):
        part = dot(taps_ref[n * 128 : n * 128 + 128], f2b_ref[9 + n])
        own = part if own is None else own + part
    own_ref[...] = own


def lower_plane_kernel(
    rim_ref, got_ref, w_ref, f2b_ref, acc_ref, own_ref, up_ref,
    yr_ref, hid_ref, taps_ref, out_ref, gp_ref,
    hs, us,
):
    inside = lax.axis_index("space") > 0
    spread_rows(rim_ref, rows_by_tap(inside), yr_ref)
    hidden = leaky(first_conv([yr_ref], w_ref[0:768]) + acc_ref[...]).astype(BF16)
    hid_ref[...] = hidden
    taps = second_taps(hidden, hs)
    for n, tap in enumerate(taps):
        taps_ref[n * 128 : n * 128 + 128] = tap
    pre = dot(jnp.concatenate(taps, axis=1), f2b_ref[0:9].reshape(1152, 128))
    pre = pre + own_ref[...] + got_ref[...] * jnp.where(inside, 1.0, 0.0)
    us[...] = up_ref[...].astype(F32).reshape(128, 128)
    up = jnp.concatenate([us[pl.ds(r, 8, stride=16), :] for r in range(16)], axis=0)
    gp_ref[...] = (up * jnp.where(pre > 0, 1.0, SLOPE)).astype(BF16)
    out_ref[...] = leaky(pre)


def second_grad(order, taps_ref, gp):
    turned = dot_nt(order, taps_ref[...]).astype(BF16)
    lhs = [turned[:, tap * 128 : tap * 128 + 128] for tap in range(9)]
    return dot(jnp.concatenate(lhs, axis=0), gp).reshape(9, 128, 128)


def lay_out(gs, at, grad):
    gs[at] = jnp.zeros((17, 16, 128), F32)
    gs[at, 0:16, 0:8, :] = grad.reshape(16, 8, 128)


def hidden_grad(gs, gu, sources, hid_ref, order):
    moved = {
        (s, dr, dq): gs[s, dr : dr + 16, dq : dq + 8, :].reshape(128, 128).astype(BF16)
        for s, _ in sources
        for dr in range(2)
        for dq in range(2)
    }
    one_d = {0: [(0, 1)], 1: [(0, 2), (1, 0)]}
    for pv in range(2):
        for pw in range(2):
            lhs, rhs = [], []
            for s, f_ref in sources:
                for dq, b in one_d[pv]:
                    for dr, c in one_d[pw]:
                        lhs.append(moved[s, dr, dq])
                        rhs.append(f_ref[3 * b + c])
            grad = dot_nt(jnp.concatenate(lhs, axis=1), jnp.concatenate(rhs, axis=1))
            grad = grad.astype(BF16).astype(F32).reshape(16, 8, 128)
            gu[:, pw, pl.ds(pv, 8, stride=2), :] = grad
    hid = hid_ref[...].astype(F32)
    grad = (gu[...].reshape(512, 128) * jnp.where(hid > 0, 1.0, SLOPE)).astype(BF16)
    return dot_nt(order, grad).astype(BF16)


def second_grad_kernel(
    low_ref, up_ref, gp_ref, pre_ref, fb_ref, hid_ref, yr_ref, y0_ref, y_ref,
    keep_ref, send_ref, out_ref, part_ref,
    os, gs, gu,
):
    order = channel_order()
    for n, taps_ref in enumerate((low_ref, up_ref)):
        grad = second_grad(order, taps_ref, gp_ref[...])
        keep_ref[9 * n : 9 * n + 9] = grad[:, :64]
        send_ref[9 * n : 9 * n + 9] = grad[:, 64:].astype(BF16)
    for r in range(16):
        os[pl.ds(r, 8, stride=16), :] = pre_ref[8 * r : 8 * r + 8]
    out_ref[...] = os[...].astype(BF16).reshape(8, 16, 128)
    lay_out(gs, 0, gp_ref[...].astype(F32))
    turned = hidden_grad(gs, gu, [(0, fb_ref.at[0:9])], hid_ref, order)
    for a, plane in enumerate((yr_ref, y0_ref, y_ref.at[0])):
        for b in range(3):
            part_ref[3 * a + b] = dot(turned, columns(plane, b))


def first_grad_kernel(
    gp_ref, gpn_ref, fa_ref, fb_ref, hid_ref, y_ref, taps_ref, part_ref,
    keep_ref, send_ref,
    gs, gu,
):
    above = gpn_ref[...].astype(F32) * jnp.where(lax.axis_index("space") < 31, 1.0, 0.0)
    lay_out(gs, 0, gp_ref[...].astype(F32))
    lay_out(gs, 1, above)
    order = channel_order()
    turned = hidden_grad(gs, gu, [(0, fb_ref.at[9:18]), (1, fa_ref)], hid_ref, order)
    low = lax.broadcasted_iota(jnp.int32, (128, 128), 1) < 64

    def put(block, grad):
        keep_ref[block] = grad[:64]
        send_ref[block] = grad[64:].astype(BF16)

    held = None
    for a in range(3):
        for b in range(3):
            ab = 3 * a + b
            grad = part_ref[ab] + dot(turned, columns(y_ref.at[a], b))
            put(ab, grad[:, 128:])
            if ab % 2 == 0:
                held = pltpu.roll(grad[:, :128], 64, axis=1)
            if ab % 2 == 1 or ab == 8:
                upper = grad[:, :128] if ab % 2 else jnp.zeros_like(held)
                put(9 + ab // 2, jnp.where(low, held, upper))
    grad = second_grad(order, taps_ref, above.astype(BF16))
    keep_ref[FIRST:] = grad[:, :64]
    send_ref[FIRST:] = grad[:, 64:].astype(BF16)


def fold_kernel(own_ref, got_ref, keep_ref, send_ref):
    total = own_ref[...] + got_ref[...].astype(F32)
    half = total.shape[1] // 2
    keep_ref[...] = total[:, :half]
    send_ref[...] = total[:, half:].astype(BF16)


def join_kernel(own_ref, got_ref, own2_ref, got2_ref, keep_ref, far_ref, s1_ref, s3_ref):
    for blocks, own, got in ((slice(0, 18), own_ref, got_ref), (slice(18, 41), own2_ref, got2_ref)):
        total = own[...] + got[...].astype(F32)
        keep_ref[blocks] = total[:, 0:4]
        s1_ref[blocks] = total[:, 4:8].astype(BF16)
        far_ref[blocks] = total[:, 8:12].astype(BF16)
        s3_ref[blocks] = total[:, 12:16].astype(BF16)


def four_kernel(far_at, own_ref, *refs):
    far_ref, a_ref, b_ref = (refs[(n + far_at) % 3] for n in range(3))
    out_ref = refs[3]
    own, far, a, b = (ref[...].astype(F32) for ref in (own_ref, far_ref, a_ref, b_ref))
    out_ref[...] = ((own + a) + (b + far)).astype(BF16)


def final_kernel(own_ref, got_ref, first_ref, second_ref):
    total = own_ref[...].astype(F32) + got_ref[...].astype(F32)
    for ab in range(9):
        first_ref[3 * ab + 1] = total[18 + ab, :, :64]
        first_ref[3 * ab + 2] = total[18 + ab, :, 64:]
        at = (ab % 2) * 64
        first_ref[3 * ab] = total[27 + ab // 2, :, at : at + 64]
    second_ref[9:27] = total[:18]
    second_ref[0:9] = total[18 + FIRST :]


VMEM, HBM = pltpu.VMEM, pltpu.HBM


def call(kernel, outs, *args, scratch=(), spaces=None, flops=10**6):
    size = sum(a.size * a.dtype.itemsize for a in args)
    spaces = spaces or [VMEM] * len(args)
    return pl.pallas_call(
        kernel,
        out_shape=[jax.ShapeDtypeStruct(shape, dtype) for shape, dtype in outs],
        in_specs=[pl.BlockSpec(memory_space=space) for space in spaces],
        out_specs=[pl.BlockSpec(memory_space=VMEM)] * len(outs),
        scratch_shapes=[pltpu.VMEM(*s) if isinstance(s, tuple) else s for s in scratch],
        compiler_params=pltpu.CompilerParams(vmem_limit_bytes=24 << 20),
        cost_estimate=pl.CostEstimate(flops=flops, bytes_accessed=size, transcendentals=0),
    )(*args)


def in_hbm(value):
    return pltpu.with_memory_space_constraint(value, HBM)


def fold(own, got):
    half = (own.shape[0], own.shape[1] // 2, 128)
    return call(fold_kernel, [(half, F32), (half, BF16)], own, got)


def local(volumes, first_filter, second_filter, upstream_grad):
    slab = in_hbm(volumes.reshape(4, 32, 4096))
    first = in_hbm(first_filter.reshape(9, 192, 128))
    second = in_hbm(second_filter.reshape(27, 128, 128))
    upstream = upstream_grad.reshape(8, 16, 128)
    y_plane = (3, 33, 16, 128)
    hs = ((17, 2, 24, 128), F32)
    tile = ((128, 128), F32)

    rim_up = volumes[0, 3]
    rim = around_space(rim_up, 1)
    y, w, second_a, hidden_up, taps_up, to_next = call(
        upper_plane_kernel,
        [
            ((3,) + y_plane, BF16), ((2304, 128), BF16), ((9, 128, 128), BF16),
            ((512, 128), BF16), ((1152, 128), BF16), tile,
        ],
        slab, rim_up, first, second, spaces=[HBM, VMEM, HBM, HBM],
        scratch=[((2, 32, 4096), BF16), ((9, 192, 128), BF16), hs, pltpu.SemaphoreType.DMA((4,))],
        flops=10**9,
    )
    from_below = around_space(to_next, 1)
    y_low, second_b, partial_low, from_up = call(
        ahead_kernel,
        [(y_plane, BF16), ((18, 128, 128), BF16), ((512, 128), F32), tile],
        slab, y, w, second, taps_up, spaces=[HBM, VMEM, VMEM, HBM, VMEM],
        scratch=[((32, 4096), BF16), pltpu.SemaphoreType.DMA((2,))], flops=10**9,
    )
    y_rim, hidden_low, taps_low, out, grad_two = call(
        lower_plane_kernel,
        [
            (y_plane, BF16), ((512, 128), BF16), ((1152, 128), BF16),
            tile, ((128, 128), BF16),
        ],
        rim, from_below, w, second_b, partial_low, from_up, upstream,
        scratch=[hs, tile], flops=4 * 10**8,
    )
    grad_two_next = around_space(grad_two, -1)
    rows = ((2, 17, 16, 128), F32)
    plane = ((16, 2, 16, 128), F32)
    keep_a, send_a, second_out, part = call(
        second_grad_kernel,
        [
            ((18, 64, 128), F32), ((18, 64, 128), BF16), ((8, 16, 128), BF16),
            ((9, 128, 256), F32),
        ],
        taps_low, taps_up, grad_two, out, second_b, hidden_low, y_rim, y_low, y,
        scratch=[tile, rows, plane], flops=8 * 10**8,
    )
    keep_b, send_b = call(
        first_grad_kernel,
        [((23, 64, 128), F32), ((23, 64, 128), BF16)],
        grad_two, grad_two_next, second_a, second_b, hidden_up, y, taps_up, part,
        scratch=[rows, plane], flops=8 * 10**8,
    )
    send_a, send_b = lax.optimization_barrier((send_a, send_b))
    keep_a, send_a = fold(keep_a, swap_core(send_a))
    keep_b, send_b = fold(keep_b, swap_core(send_b))
    keep_a, send_a = fold(keep_a, swap_x(send_a, 0))
    keep_b, send_b = fold(keep_b, swap_x(send_b, 0))
    part = (FIRST + SECOND, 4, 128)
    keep, far, one, three = call(
        join_kernel, [(part, F32), (part, BF16), (part, BF16), (part, BF16)],
        keep_a, swap_x(send_a, 1), keep_b, swap_x(send_b, 1),
    )
    (both,) = call(
        functools.partial(four_kernel, 1), [(part, BF16)],
        keep, swap_z(one, 1), swap_z(far, 2), swap_z(three, 3),
    )
    (both,) = call(
        functools.partial(four_kernel, 0), [(part, BF16)],
        both, swap_y(both, 2), swap_y(both, 1), swap_y(both, 3),
    )
    first_grad, second_grad = call(
        final_kernel,
        [((27, 4, 64), F32), ((27, 4, 128), F32)],
        both, swap_z_low(both),
    )
    return (
        second_out.reshape(1, 1, 8, 16, 128),
        jnp.swapaxes(first_grad, 1, 2).reshape(3, 3, 3, 64, 4),
        second_grad.reshape(3, 3, 3, 4, 128),
    )


def solution(mesh):
    placed = (P("dp", "space", None, None), P(), P(), P("dp", "space", None, None, None))
    return jax.shard_map(
        local,
        mesh=mesh,
        in_specs=placed,
        out_specs=(
            P("dp", "space", None, None, None),
            P(None, None, None, None, "space"),
            P(None, None, None, "space", None),
        ),
        check_vma=False,
    )
```

```python
import functools

import jax
import jax.numpy as jnp
from jax import lax
from jax.experimental import pallas as pl
from jax.experimental.pallas import tpu as pltpu
from jax.sharding import PartitionSpec as P

SLOPE = 0.3
F32, BF16 = jnp.float32, jnp.bfloat16
FIRST, SECOND = 14, 27


def around_space(value, by):
    return lax.ppermute(value, "space", [(i, (i + by) % 32) for i in range(32)])


def swap_core(value):
    return lax.ppermute(value, "space", [(i, i ^ 1) for i in range(32)])


def partner(step, core):
    return 1 if (step + core) % 2 == 0 else 3


def swap_x(value, step):
    return lax.ppermute(value, "space", [(s, s ^ (partner(step, s & 1) << 3)) for s in range(32)])


def swap_z(value, slot):
    return lax.ppermute(value, "space", [(s, s ^ (slot << 1)) for s in range(32)])


def swap_y(value, slot):
    return lax.ppermute(value, "dp", [(d, d ^ slot) for d in range(8)])


def swap_z_low(value):
    return lax.ppermute(value, "dp", [(d, d ^ 4) for d in range(8)])


def leaky(values):
    return jnp.where(values > 0, values, SLOPE * values)


def dot(a, b):
    return jnp.dot(a, b, preferred_element_type=F32)


def dot_nt(a, b):
    return lax.dot_general(a, b, (((1,), (1,)), ((), ())), preferred_element_type=F32)


def rows_by_tap(keep=None):
    m = lax.broadcasted_iota(jnp.int32, (48, 32), 0)
    h = lax.broadcasted_iota(jnp.int32, (48, 32), 1)
    picked = h == 2 * (m & 15) + (m >> 4) - 1
    if keep is not None:
        picked = jnp.logical_and(picked, keep)
    return jnp.where(picked, 1.0, 0.0).astype(BF16)


def channel_order():
    s = lax.axis_index("space")
    m = lax.broadcasted_iota(jnp.int32, (128, 128), 0)
    i = lax.broadcasted_iota(jnp.int32, (128, 128), 1)
    core = (m >> 6) ^ (s & 1)
    near, far = 1 + 2 * core, 3 - 2 * core
    x = (near * ((m >> 5) & 1)) ^ (far * ((m >> 4) & 1)) ^ (s >> 3)
    z = ((m >> 2) & 3) ^ ((s >> 1) & 3)
    return jnp.where(i == x * 32 + z * 8 + core * 4 + (m & 3), 1.0, 0.0).astype(BF16)


def spread_rows(plane_ref, pick, y_ref):
    for t in range(3):
        y_ref[t, 0] = jnp.zeros((16, 128), BF16)
    for n in range(8):
        out = dot(pick, plane_ref[:, n * 512 : (n + 1) * 512]).astype(BF16)
        for t in range(3):
            for r in range(4):
                y_ref[t, 1 + 4 * n + r] = out[16 * t : 16 * t + 16, 128 * r : 128 * r + 128]


def columns(y_ref, b):
    before = y_ref[b, 0:32].reshape(512, 128)
    at = y_ref[b, 1:33].reshape(512, 128)
    return jnp.concatenate([before, at], axis=1)


def first_conv(planes, w):
    lhs = jnp.concatenate([columns(plane, b) for plane in planes for b in range(3)], axis=1)
    return dot(lhs, w)


def second_taps(hidden, hs):
    h = hidden.astype(F32).reshape(16, 2, 16, 128)
    hs[:, :, 0:8, :] = jnp.zeros((17, 2, 8, 128), F32)
    hs[0, 0] = jnp.zeros((24, 128), F32)
    hs[0:16, 1, 8:24, :] = h[:, 0]
    hs[1:17, 0, 8:24, :] = h[:, 1]
    taps = []
    for b in range(3):
        for c in range(3):
            rows = hs[c // 2 : c // 2 + 16, c % 2, pl.ds(7 + b, 8, stride=2), :]
            taps.append(rows.reshape(128, 128).astype(BF16))
    return taps


def upper_plane_kernel(
    v_ref, rim_ref, f_ref, f2_ref,
    y_ref, w_ref, f2a_ref, hid_ref, taps_ref, next_ref,
    v, f, hs, sems,
):
    copies = [
        pltpu.make_async_copy(v_ref.at[1], v.at[0], sems.at[0]),
        pltpu.make_async_copy(v_ref.at[2], v.at[1], sems.at[1]),
        pltpu.make_async_copy(f_ref, f, sems.at[2]),
        pltpu.make_async_copy(f2_ref.at[0:9], f2a_ref, sems.at[3]),
    ]
    for copy in copies:
        copy.start()
    pick = rows_by_tap()
    spread_rows(rim_ref, pick, y_ref.at[2])
    for p in range(2):
        copies[p].wait()
        spread_rows(v.at[p], pick, y_ref.at[p])
    copies[2].wait()
    for ab in range(9):
        w_ref[ab * 256 : ab * 256 + 64] = jnp.zeros((64, 128), BF16)
        w_ref[ab * 256 + 64 : ab * 256 + 256] = f[ab]
    hidden = leaky(first_conv([y_ref.at[p] for p in range(3)], w_ref[...])).astype(BF16)
    hid_ref[...] = hidden
    taps = second_taps(hidden, hs)
    for n, tap in enumerate(taps):
        taps_ref[n * 128 : n * 128 + 128] = tap
    copies[3].wait()
    next_ref[...] = dot(jnp.concatenate(taps, axis=1), f2a_ref[...].reshape(1152, 128))


def ahead_kernel(
    v_ref, y_ref, w_ref, f2_ref, taps_ref, y0_ref, f2b_ref, acc_ref, own_ref, v, sems
):
    copies = [
        pltpu.make_async_copy(v_ref.at[0], v, sems.at[0]),
        pltpu.make_async_copy(f2_ref.at[9:27], f2b_ref, sems.at[1]),
    ]
    for copy in copies:
        copy.start()
    copies[0].wait()
    spread_rows(v, rows_by_tap(), y0_ref)
    acc_ref[...] = first_conv([y0_ref, y_ref.at[0]], w_ref[768:])
    copies[1].wait()
    own = None
    for n in range(9):
        part = dot(taps_ref[n * 128 : n * 128 + 128], f2b_ref[9 + n])
        own = part if own is None else own + part
    own_ref[...] = own


def lower_plane_kernel(
    rim_ref, got_ref, w_ref, f2b_ref, acc_ref, own_ref, up_ref,
    yr_ref, hid_ref, taps_ref, out_ref, gp_ref,
    hs, us,
):
    inside = lax.axis_index("space") > 0
    spread_rows(rim_ref, rows_by_tap(inside), yr_ref)
    hidden = leaky(first_conv([yr_ref], w_ref[0:768]) + acc_ref[...]).astype(BF16)
    hid_ref[...] = hidden
    taps = second_taps(hidden, hs)
    for n, tap in enumerate(taps):
        taps_ref[n * 128 : n * 128 + 128] = tap
    pre = dot(jnp.concatenate(taps, axis=1), f2b_ref[0:9].reshape(1152, 128))
    pre = pre + own_ref[...] + got_ref[...] * jnp.where(inside, 1.0, 0.0)
    us[...] = up_ref[...].astype(F32).reshape(128, 128)
    up = jnp.concatenate([us[pl.ds(r, 8, stride=16), :] for r in range(16)], axis=0)
    gp_ref[...] = (up * jnp.where(pre > 0, 1.0, SLOPE)).astype(BF16)
    out_ref[...] = leaky(pre)


def second_grad(turned, gp):
    lhs = [turned[:, tap * 128 : tap * 128 + 128] for tap in range(9)]
    return dot(jnp.concatenate(lhs, axis=0), gp).reshape(9, 128, 128)


def lay_out(gs, at, grad):
    gs[at] = jnp.zeros((17, 16, 128), F32)
    gs[at, 0:16, 0:8, :] = grad.reshape(16, 8, 128)


def class_sums(gs, sources):
    moved = {
        (s, dr, dq): gs[s, dr : dr + 16, dq : dq + 8, :].reshape(128, 128).astype(BF16)
        for s, _ in sources
        for dr in range(2)
        for dq in range(2)
    }
    one_d = {0: [(0, 1)], 1: [(0, 2), (1, 0)]}
    sums = []
    for pv in range(2):
        for pw in range(2):
            lhs, rhs = [], []
            for s, f_ref in sources:
                for dq, b in one_d[pv]:
                    for dr, c in one_d[pw]:
                        lhs.append(moved[s, dr, dq])
                        rhs.append(f_ref[3 * b + c])
            sums.append(dot_nt(jnp.concatenate(lhs, axis=1), jnp.concatenate(rhs, axis=1)))
    return sums


def hidden_grad(gu, sums, hid_ref, order):
    for n, grad in enumerate(sums):
        grad = grad.astype(BF16).astype(F32).reshape(16, 8, 128)
        gu[:, n % 2, pl.ds(n // 2, 8, stride=2), :] = grad
    hid = hid_ref[...].astype(F32)
    grad = (gu[...].reshape(512, 128) * jnp.where(hid > 0, 1.0, SLOPE)).astype(BF16)
    return dot_nt(order, grad).astype(BF16)


def second_grad_kernel(
    low_ref, up_ref, gp_ref, pre_ref, fb_ref, hid_ref, yr_ref, y0_ref, y_ref,
    keep_ref, send_ref, out_ref, part_ref, turned_ref, lead_ref,
    os, gs, gu,
):
    order = channel_order()
    for n, taps_ref in enumerate((low_ref, up_ref)):
        turned = dot_nt(order, taps_ref[...]).astype(BF16)
        grad = second_grad(turned, gp_ref[...])
        keep_ref[9 * n : 9 * n + 9] = grad[:, :64]
        send_ref[9 * n : 9 * n + 9] = grad[:, 64:].astype(BF16)
    turned_ref[...] = turned
    for r in range(16):
        os[pl.ds(r, 8, stride=16), :] = pre_ref[8 * r : 8 * r + 8]
    out_ref[...] = os[...].astype(BF16).reshape(8, 16, 128)
    lay_out(gs, 0, gp_ref[...].astype(F32))
    turned = hidden_grad(gu, class_sums(gs, [(0, fb_ref.at[0:9])]), hid_ref, order)
    for n, grad in enumerate(class_sums(gs, [(0, fb_ref.at[9:18])])):
        lead_ref[n] = grad
    for a, plane in enumerate((yr_ref, y0_ref, y_ref.at[0])):
        for b in range(3):
            part_ref[3 * a + b] = dot(turned, columns(plane, b))


def first_grad_kernel(
    gpn_ref, fa_ref, hid_ref, y_ref, turned_ref, part_ref, lead_ref,
    keep_ref, send_ref,
    gs, gu,
):
    above = gpn_ref[...].astype(F32) * jnp.where(lax.axis_index("space") < 31, 1.0, 0.0)
    lay_out(gs, 0, above)
    sums = [lead_ref[n] + grad for n, grad in enumerate(class_sums(gs, [(0, fa_ref)]))]
    turned = hidden_grad(gu, sums, hid_ref, channel_order())
    low = lax.broadcasted_iota(jnp.int32, (128, 128), 1) < 64

    def put(block, grad):
        keep_ref[block] = grad[:64]
        send_ref[block] = grad[64:].astype(BF16)

    held = None
    for a in range(3):
        for b in range(3):
            ab = 3 * a + b
            grad = part_ref[ab] + dot(turned, columns(y_ref.at[a], b))
            put(ab, grad[:, 128:])
            if ab % 2 == 0:
                held = pltpu.roll(grad[:, :128], 64, axis=1)
            if ab % 2 == 1 or ab == 8:
                upper = grad[:, :128] if ab % 2 else jnp.zeros_like(held)
                put(9 + ab // 2, jnp.where(low, held, upper))
    grad = second_grad(turned_ref[...], above.astype(BF16))
    keep_ref[FIRST:] = grad[:, :64]
    send_ref[FIRST:] = grad[:, 64:].astype(BF16)


def fold_kernel(own_ref, got_ref, keep_ref, send_ref):
    total = own_ref[...] + got_ref[...].astype(F32)
    half = total.shape[1] // 2
    keep_ref[...] = total[:, :half]
    send_ref[...] = total[:, half:].astype(BF16)


def join_kernel(own_ref, got_ref, own2_ref, got2_ref, keep_ref, far_ref, s1_ref, s3_ref):
    for blocks, own, got in ((slice(0, 18), own_ref, got_ref), (slice(18, 41), own2_ref, got2_ref)):
        total = own[...] + got[...].astype(F32)
        keep_ref[blocks] = total[:, 0:4]
        s1_ref[blocks] = total[:, 4:8].astype(BF16)
        far_ref[blocks] = total[:, 8:12].astype(BF16)
        s3_ref[blocks] = total[:, 12:16].astype(BF16)


def four_kernel(far_at, own_ref, *refs):
    far_ref, a_ref, b_ref = (refs[(n + far_at) % 3] for n in range(3))
    out_ref = refs[3]
    own, far, a, b = (ref[...].astype(F32) for ref in (own_ref, far_ref, a_ref, b_ref))
    out_ref[...] = ((own + a) + (b + far)).astype(BF16)


def final_kernel(own_ref, got_ref, first_ref, second_ref):
    total = own_ref[...].astype(F32) + got_ref[...].astype(F32)
    for ab in range(9):
        first_ref[3 * ab + 1] = total[18 + ab, :, :64]
        first_ref[3 * ab + 2] = total[18 + ab, :, 64:]
        at = (ab % 2) * 64
        first_ref[3 * ab] = total[27 + ab // 2, :, at : at + 64]
    second_ref[9:27] = total[:18]
    second_ref[0:9] = total[18 + FIRST :]


VMEM, HBM = pltpu.VMEM, pltpu.HBM


def call(kernel, outs, *args, scratch=(), spaces=None, flops=10**6):
    size = sum(a.size * a.dtype.itemsize for a in args)
    spaces = spaces or [VMEM] * len(args)
    return pl.pallas_call(
        kernel,
        out_shape=[jax.ShapeDtypeStruct(shape, dtype) for shape, dtype in outs],
        in_specs=[pl.BlockSpec(memory_space=space) for space in spaces],
        out_specs=[pl.BlockSpec(memory_space=VMEM)] * len(outs),
        scratch_shapes=[pltpu.VMEM(*s) if isinstance(s, tuple) else s for s in scratch],
        compiler_params=pltpu.CompilerParams(vmem_limit_bytes=24 << 20),
        cost_estimate=pl.CostEstimate(flops=flops, bytes_accessed=size, transcendentals=0),
    )(*args)


def in_hbm(value):
    return pltpu.with_memory_space_constraint(value, HBM)


def fold(own, got):
    half = (own.shape[0], own.shape[1] // 2, 128)
    return call(fold_kernel, [(half, F32), (half, BF16)], own, got)


def local(volumes, first_filter, second_filter, upstream_grad):
    slab = in_hbm(volumes.reshape(4, 32, 4096))
    first = in_hbm(first_filter.reshape(9, 192, 128))
    second = in_hbm(second_filter.reshape(27, 128, 128))
    upstream = upstream_grad.reshape(8, 16, 128)
    y_plane = (3, 33, 16, 128)
    hs = ((17, 2, 24, 128), F32)
    tile = ((128, 128), F32)

    rim_up = volumes[0, 3]
    rim = around_space(rim_up, 1)
    y, w, second_a, hidden_up, taps_up, to_next = call(
        upper_plane_kernel,
        [
            ((3,) + y_plane, BF16), ((2304, 128), BF16), ((9, 128, 128), BF16),
            ((512, 128), BF16), ((1152, 128), BF16), tile,
        ],
        slab, rim_up, first, second, spaces=[HBM, VMEM, HBM, HBM],
        scratch=[((2, 32, 4096), BF16), ((9, 192, 128), BF16), hs, pltpu.SemaphoreType.DMA((4,))],
        flops=10**9,
    )
    from_below = around_space(to_next, 1)
    y_low, second_b, partial_low, from_up = call(
        ahead_kernel,
        [(y_plane, BF16), ((18, 128, 128), BF16), ((512, 128), F32), tile],
        slab, y, w, second, taps_up, spaces=[HBM, VMEM, VMEM, HBM, VMEM],
        scratch=[((32, 4096), BF16), pltpu.SemaphoreType.DMA((2,))], flops=10**9,
    )
    y_rim, hidden_low, taps_low, out, grad_two = call(
        lower_plane_kernel,
        [
            (y_plane, BF16), ((512, 128), BF16), ((1152, 128), BF16),
            tile, ((128, 128), BF16),
        ],
        rim, from_below, w, second_b, partial_low, from_up, upstream,
        scratch=[hs, tile], flops=4 * 10**8,
    )
    grad_two_next = around_space(grad_two, -1)
    rows = ((1, 17, 16, 128), F32)
    plane = ((16, 2, 16, 128), F32)
    keep_a, send_a, second_out, part, turned, lead = call(
        second_grad_kernel,
        [
            ((18, 64, 128), F32), ((18, 64, 128), BF16), ((8, 16, 128), BF16),
            ((9, 128, 256), F32), ((128, 1152), BF16), ((4, 128, 128), F32),
        ],
        taps_low, taps_up, grad_two, out, second_b, hidden_low, y_rim, y_low, y,
        scratch=[tile, rows, plane], flops=8 * 10**8,
    )
    keep_b, send_b = call(
        first_grad_kernel,
        [((23, 64, 128), F32), ((23, 64, 128), BF16)],
        grad_two_next, second_a, hidden_up, y, turned, part, lead,
        scratch=[rows, plane], flops=8 * 10**8,
    )
    send_a, send_b = lax.optimization_barrier((send_a, send_b))
    keep_a, send_a = fold(keep_a, swap_core(send_a))
    keep_b, send_b = fold(keep_b, swap_core(send_b))
    keep_a, send_a = fold(keep_a, swap_x(send_a, 0))
    keep_b, send_b = fold(keep_b, swap_x(send_b, 0))
    part = (FIRST + SECOND, 4, 128)
    keep, far, one, three = call(
        join_kernel, [(part, F32), (part, BF16), (part, BF16), (part, BF16)],
        keep_a, swap_x(send_a, 1), keep_b, swap_x(send_b, 1),
    )
    (both,) = call(
        functools.partial(four_kernel, 1), [(part, BF16)],
        keep, swap_z(one, 1), swap_z(far, 2), swap_z(three, 3),
    )
    (both,) = call(
        functools.partial(four_kernel, 0), [(part, BF16)],
        both, swap_y(both, 2), swap_y(both, 1), swap_y(both, 3),
    )
    first_grad, second_grad = call(
        final_kernel,
        [((27, 4, 64), F32), ((27, 4, 128), F32)],
        both, swap_z_low(both),
    )
    return (
        second_out.reshape(1, 1, 8, 16, 128),
        jnp.swapaxes(first_grad, 1, 2).reshape(3, 3, 3, 64, 4),
        second_grad.reshape(3, 3, 3, 4, 128),
    )


def solution(mesh):
    placed = (P("dp", "space", None, None), P(), P(), P("dp", "space", None, None, None))
    return jax.shard_map(
        local,
        mesh=mesh,
        in_specs=placed,
        out_specs=(
            P("dp", "space", None, None, None),
            P(None, None, None, None, "space"),
            P(None, None, None, "space", None),
        ),
        check_vma=False,
    )
```
